128 devices in a mesh: section: 2 (over core), row: 16 (over z, y), col: 4 (over x).
Axes of the slice: x: 4, y: 4, z: 4, core: 2. Of those that a mesh axis runs over, the one named last changes fastest.
Arguments:
- queries: bfloat16 [16384, 4096], P(('section', 'col'), 'row'), may hold values from -8 to 8
- keys: bfloat16 [16384, 512], P(('section', 'col')), may hold values from -6 to 6
- values: bfloat16 [16384, 512], P(('section', 'col')), may hold values from -6 to 6
- out_grad: bfloat16 [16384, 4096], P(('section', 'col'), 'row'), may hold values from -12 to 12
- q_weight: bfloat16 [2048, 4096], P('col', 'row'), may hold values from -0.125 to 0.125
- k_weight: bfloat16 [2048, 512], P('col'), may hold values from -0.125 to 0.125
- v_weight: bfloat16 [2048, 512], P('col'), may hold values from -0.125 to 0.125
- resid_grad: bfloat16 [16384, 2048], P(('section', 'row', 'col')), may hold values from -4 to 4
- moe_input: bfloat16 [16384, 2048], P(('section', 'row', 'col')), may hold values from -6 to 6
- expert_ids: int32 [16384, 8], P(('section', 'row', 'col')), may hold values from 0 to 127, all different within a row; in each aligned block of 128 rows (0 to 127, 128 to 255, ...) at most 9 rows name the same one
- route_weights: float32 [16384, 8], P(('section', 'row', 'col')), may hold values from 0.03 to 0.4
- w_gate_up: bfloat16 [128, 2048, 1536], P(('section', 'row', 'col')), may hold values from -0.125 to 0.125
- w_down: bfloat16 [128, 768, 2048], P(('section', 'row', 'col')), may hold values from -0.21875 to 0.21875
Outputs:
- moe_input_grad: bfloat16 [16384, 2048], P(('section', 'row', 'col'))
The draws below stay inside these ranges and needn't reach their ends.
Inputs may be any that keep to these rules, and one draw needn't show every extreme that they name: `expert_ids`: each row names 8 different experts; among the rows of one device no expert is named by more than 9 rows, and in every draw some expert is named by exactly 9 rows of some device.
All inputs are finite; a program needn't handle non-finite values.
Results may differ from the reference program's by a relative error of at most 0.02.
Values may be sent and summed in bfloat16 or wider, within the bound.
No kernel may reach another device: no remote copies, remote signals or barrier semaphores. Data moves between devices by JAX's collectives and lax.ppermute only.
A program may use at most 128 MiB of HBM per device.

```python
import math
import jax
import jax.numpy as jnp
import numpy as np
from jax import lax

D = 2048
HEADS = 32
KV_HEADS = 4
HEAD_DIM = 128
EXP_FF = 768
TOPK = 8
DOC = 1024
EXPERTS = 128
TOK_MOE = 128
TOKENS = 16384
HQ_DEV = 2
CAP = 9
N_ROW = 16
N_COL = 4


def draw_keys(key, part):
    shape = (TOKENS, KV_HEADS * HEAD_DIM)
    base = jnp.clip(jax.random.normal(jax.random.fold_in(key, 11), shape, jnp.float32), -6.0, 6.0)
    return base.astype(jnp.bfloat16)


def draw_queries(key, part):
    shape = (TOKENS, HEADS * HEAD_DIM)
    base = jnp.clip(jax.random.normal(jax.random.fold_in(key, 21), shape, jnp.float32), -6.0, 6.0)
    return base.astype(jnp.bfloat16)


def level_of(own_key, shape, pieces, least, high):
    factor_of, own = 1.0, jax.random.fold_in(own_key, 6)
    for dim, blocks in pieces:
        draws = jnp.exp(jax.random.uniform(jax.random.fold_in(own, dim), (blocks,), jnp.float32, least / len(pieces), high / len(pieces)))
        factor_of = factor_of * jnp.repeat(draws, shape[dim] // blocks).reshape([-1 if axis == dim else 1 for axis in range(len(shape))])
    return factor_of


def assign_block(key, own, number, rows, amount, top, most, slope):
    ranking = jax.random.permutation(key, amount)
    heavy_load, ordinary = shares(amount, rows * top, most, slope, True), shares(amount, rows * top, most, slope, False)
    places = jnp.arange(amount)

    def named(sizes, offset_by):
        used = int((sizes > 0).sum())
        fixed = max(1, used // 4)
        moved = fixed + (places - fixed + offset_by * (used - fixed)) % max(1, amount - fixed)
        return jnp.zeros((amount,), jnp.int32).at[ranking[jnp.where(places < fixed, places, moved)]].set(jnp.asarray(sizes, jnp.int32))

    sizes = jnp.where(number % 4 == 0, named(heavy_load, number // 4), named(ordinary, number - number // 4 - 1))
    mixed = jax.random.permutation(jax.random.fold_in(own, 3), amount)
    giver, sink = mixed[0:amount // 2 * 2:2], mixed[1:amount // 2 * 2:2]
    margin = jnp.minimum(sizes[giver] - 1, most - sizes[sink]) // 2
    margin = jnp.where((giver == ranking[0]) | (sink == ranking[0]) | (sizes[sink] == 0), 0, jnp.maximum(margin, 0))
    moved = jax.random.randint(jax.random.fold_in(own, 4), (amount // 2,), 0, 1 << 20) % (margin + 1)
    sizes = sizes.at[giver].add(-moved).at[sink].add(moved)
    items = jnp.searchsorted(jnp.cumsum(sizes), jnp.arange(rows * top), side="right").astype(jnp.int32)
    grid = items.reshape(top, rows).T
    grid = grid[jax.random.permutation(jax.random.fold_in(own, 1), rows)]
    offset_by = jax.random.randint(jax.random.fold_in(own, 2), (rows, 1), 0, top)
    return jnp.take_along_axis(grid, (jnp.arange(top)[None, :] + offset_by) % top, axis=1)


def shares(number_of, total, most, skew, full):
    portions = [(1 << 20) // math.isqrt(rank ** skew) + 1 for rank in range(1, number_of + 1)]
    largest = most if full else min(most, max(-(-total // number_of), total * portions[0] // sum(portions)))
    least = 1 if total - largest >= number_of - 1 else 0
    counts, spare = [largest] + [least] * (number_of - 1), total - largest - least * (number_of - 1)
    while spare > 0:
        movable = [i for i in range(1, number_of) if counts[i] < largest] or [i for i in range(1, number_of) if counts[i] < most]
        whole, left = sum([portions[i] for i in movable]), spare
        for i in movable:
            extra = min(most - counts[i], max(1, left * portions[i] // whole), spare)
            counts[i] = counts[i] + extra
            spare = spare - extra
    return np.array(counts)


def scatter_about(rng, extent, scale, most, cuts=(), held_as=jnp.bfloat16):
    values = jax.random.normal(rng, extent, jnp.float32) * scale
    if len(cuts) > 0:
        values = level_of(rng, extent, cuts, -0.22, 0.18) * values
    return jnp.clip(values, min=-most, max=most).astype(held_as)


def setup_inputs(seed: int = 0) -> dict:
    seeds = jax.random.split(jax.random.key(seed), 14)
    queries = draw_queries(jax.random.fold_in(seeds[13], 71), 0)
    keys = draw_keys(jax.random.fold_in(seeds[13], 71), 0)
    values = scatter_about(seeds[2], (TOKENS, KV_HEADS * HEAD_DIM), 1.0, 6.0, ((0, 8),))
    out_grad = scatter_about(seeds[3], (TOKENS, HEADS * HEAD_DIM), 2.0, 12.0, ((0, 8), (1, 16)))
    q_weight = scatter_about(seeds[4], (D, HEADS * HEAD_DIM), D ** -0.5, 0.125, ((0, 4), (1, 16)))
    k_weight = scatter_about(seeds[5], (D, KV_HEADS * HEAD_DIM), D ** -0.5, 0.125, ((0, 4),))
    v_weight = scatter_about(seeds[6], (D, KV_HEADS * HEAD_DIM), D ** -0.5, 0.125, ((0, 4),))
    resid_grad = scatter_about(seeds[7], (TOKENS, D), 0.5, 4.0, ((0, 128),))
    moe_input = scatter_about(seeds[8], (TOKENS, D), 1.0, 6.0, ((0, 128),))
    expert_ids_keys = jax.random.split(jax.random.fold_in(seeds[9], 1), TOKENS // TOK_MOE)
    expert_ids_turns = jax.random.permutation(jax.random.fold_in(seeds[9], 3), TOKENS // TOK_MOE)
    expert_ids = jax.vmap(lambda own, number: assign_block(jax.random.fold_in(seeds[9], 2), own, number, TOK_MOE, EXPERTS, TOPK, CAP, 2))(expert_ids_keys, expert_ids_turns).reshape((TOKENS, TOPK))
    route_weights = jnp.clip(jnp.exp(math.log(0.4) - 2.5902672 * jax.random.uniform(seeds[10], (TOKENS, TOPK), jnp.float32) ** level_of(seeds[10], (TOKENS, TOPK), ((0, 128),), -0.2, 0.2)), 0.03, 0.4)
    w_gate_up = scatter_about(seeds[11], (EXPERTS, D, 2 * EXP_FF), D ** -0.5, 0.125, ((0, 128),))
    w_down = scatter_about(seeds[12], (EXPERTS, EXP_FF, D), EXP_FF ** -0.5, 0.21875, ((0, 128),))
    return {"queries": queries, "keys": keys, "values": values, "out_grad": out_grad, "q_weight": q_weight, "k_weight": k_weight, "v_weight": v_weight, "resid_grad": resid_grad, "moe_input": moe_input, "expert_ids": expert_ids, "route_weights": route_weights, "w_gate_up": w_gate_up, "w_down": w_down}


def expert_math(rows_in, grad_in, w_gu, w_dn):
    width = w_dn.shape[0]
    gate_up = jnp.dot(rows_in, w_gu, preferred_element_type=jnp.float32)
    gate = gate_up[:, :width]
    up_part = gate_up[:, width:]
    dhidden = lax.dot_general(grad_in, w_dn, (((1,), (1,)), ((), ())), preferred_element_type=jnp.float32)
    sigm = jax.nn.sigmoid(gate)
    d_gate = dhidden * up_part * sigm * (1.0 + gate * (1.0 - sigm))
    d_up = dhidden * gate * sigm
    dgate_up = jnp.concatenate([d_gate, d_up], axis=1).astype(jnp.bfloat16)
    back_rows = lax.dot_general(dgate_up, w_gu, (((1,), (1,)), ((), ())), preferred_element_type=jnp.float32)
    return back_rows.astype(jnp.bfloat16)


def reference(queries, keys, values, out_grad, q_weight, k_weight, v_weight, resid_grad, moe_input, expert_ids, route_weights, w_gate_up, w_down):
    group_size = HEADS // KV_HEADS
    num_docs = TOKENS // DOC
    section_total = TOKENS // (N_ROW * N_COL * TOK_MOE)
    scale_val = HEAD_DIM ** -0.5
    qd = queries.reshape(num_docs, DOC, HEADS, HEAD_DIM)
    od = out_grad.reshape(num_docs, DOC, HEADS, HEAD_DIM)
    kd = keys.reshape(num_docs, DOC, KV_HEADS, HEAD_DIM)
    vd = values.reshape(num_docs, DOC, KV_HEADS, HEAD_DIM)
    kv_of_group = (jnp.arange(N_ROW) * HQ_DEV) // group_size
    wq_groups = jnp.transpose(q_weight.reshape(D, N_ROW, HQ_DEV * HEAD_DIM), (1, 0, 2))
    wk_groups = jnp.transpose(k_weight.reshape(D, KV_HEADS, HEAD_DIM)[:, kv_of_group], (1, 0, 2))
    wv_groups = jnp.transpose(v_weight.reshape(D, KV_HEADS, HEAD_DIM)[:, kv_of_group], (1, 0, 2))
    wcat_groups = jnp.concatenate([wq_groups, wk_groups, wv_groups], axis=2).astype(jnp.float32)
    causal = jnp.arange(DOC)[:, None] >= jnp.arange(DOC)[None, :]

    def one_doc(block):
        query_blk, grad_blk, key_blk, value_blk = block
        key_rep = jnp.repeat(key_blk, group_size, axis=1).astype(jnp.float32)
        value_rep = jnp.repeat(value_blk, group_size, axis=1).astype(jnp.float32)
        query_f = query_blk.astype(jnp.float32)
        grad_f = grad_blk.astype(jnp.float32)
        scores = jnp.einsum('qhd,khd->hqk', query_f, key_rep) * scale_val
        scores = jnp.where(causal[None], scores, -jnp.inf)
        top = jnp.max(scores, axis=-1, keepdims=True)
        expo = jnp.exp(scores - top)
        probs = expo / jnp.sum(expo, axis=-1, keepdims=True)
        probs_b = probs.astype(jnp.bfloat16)
        dprob = jnp.einsum('qhd,khd->hqk', grad_f, value_rep)
        delta = jnp.sum(probs * dprob, axis=-1, keepdims=True)
        dscore = (probs * (dprob - delta)).astype(jnp.bfloat16)
        dscore_f = dscore.astype(jnp.float32)
        dquery = (jnp.einsum('hqk,khd->qhd', dscore_f, key_rep) * scale_val).astype(jnp.bfloat16)
        dscore_g = dscore_f.reshape(N_ROW, HQ_DEV, DOC, DOC)
        probs_g = probs_b.astype(jnp.float32).reshape(N_ROW, HQ_DEV, DOC, DOC)
        query_g = query_f.reshape(DOC, N_ROW, HQ_DEV, HEAD_DIM)
        grad_g = grad_f.reshape(DOC, N_ROW, HQ_DEV, HEAD_DIM)
        dkey = (jnp.einsum('ghqk,qghd->gkd', dscore_g, query_g) * scale_val).astype(jnp.bfloat16)
        dvalue = jnp.einsum('ghqk,qghd->gkd', probs_g, grad_g).astype(jnp.bfloat16)
        dquery_g = jnp.transpose(dquery.reshape(DOC, N_ROW, HQ_DEV * HEAD_DIM), (1, 0, 2))
        dqkv = jnp.concatenate([dquery_g, dkey, dvalue], axis=2).astype(jnp.float32)
        part = jnp.einsum('gtc,gdc->gtd', dqkv, wcat_groups)
        part = lax.optimization_barrier(part.astype(jnp.bfloat16)).astype(jnp.float32)
        return jnp.sum(part, axis=0)

    head_grad = lax.map(one_doc, (qd, od, kd, vd))
    head_grad = head_grad.reshape(section_total, N_COL, N_ROW, TOK_MOE, D)
    head_grad = jnp.transpose(head_grad, (0, 2, 1, 3, 4)).reshape(TOKENS, D)
    layer_grad = head_grad + resid_grad.astype(jnp.float32)
    row_grad = layer_grad.astype(jnp.bfloat16)

    limit = EXPERTS * CAP
    rows_pad = jnp.concatenate([moe_input, jnp.zeros((1, D), jnp.bfloat16)], axis=0)
    grads_pad = jnp.concatenate([row_grad, jnp.zeros((1, D), jnp.bfloat16)], axis=0)

    def per_expert(carry, expert):
        hits = expert_ids == expert
        weight = jnp.sum(jnp.where(hits, route_weights, jnp.zeros_like(route_weights)), axis=1)
        weight_pad = jnp.concatenate([weight, jnp.zeros((1,), weight.dtype)], axis=0)
        chosen = jnp.any(hits, axis=1)
        index_list = jnp.nonzero(chosen, size=limit, fill_value=TOKENS)[0].astype(jnp.int32)
        result = expert_math(rows_pad[index_list], grads_pad[index_list], w_gate_up[expert], w_down[expert])
        carry = carry.at[index_list].add(weight_pad[index_list][:, None] * result.astype(jnp.float32))
        return carry, None

    start = jnp.zeros((TOKENS + 1, D), jnp.float32)
    total, unused = lax.scan(per_expert, start, jnp.arange(EXPERTS, dtype=jnp.int32))
    return total[:TOKENS].astype(jnp.bfloat16)
```

```python
import math

import jax
import jax.numpy as jnp
from jax import lax
from jax.experimental import pallas as pl
from jax.experimental.pallas import tpu as pltpu
from jax.sharding import PartitionSpec as P

HEADS = 32
KV_HEADS = 4
HD = 128
TOPK = 8
DOC = 1024
D = 2048
FF = 768
CAP = 9
TOK = 128
NE = 128
N_Y = 4
N_Z = 4
HALF = 1024
MSG = 72
CHUNK = 32
ROWS = CHUNK * CAP
BF = jnp.bfloat16
F32 = jnp.float32
VMEM_LIMIT = 60 * 1024 * 1024
ALL = ("section", "row", "col")
SCALE = HD ** (-0.5)


def params(steps):
    return pltpu.CompilerParams(
        dimension_semantics=("arbitrary",) * steps, vmem_limit_bytes=VMEM_LIMIT
    )


def dot_nn(a, b):
    return lax.dot_general(a, b, (((1,), (0,)), ((), ())), preferred_element_type=F32)


def dot_nt(a, b):
    return lax.dot_general(a, b, (((1,), (1,)), ((), ())), preferred_element_type=F32)


def pack_half(x, pick, out_ref, scr):
    main = pick[: NE * 8]
    last = pick[NE * 8 :]
    for jj in range(0, 8, 2):
        got = dot_nn(main, x[:, jj * 128 : (jj + 2) * 128])
        for q in range(2):
            piece = got[:, q * 128 : (q + 1) * 128].reshape(NE, 8, 128)
            out_ref[:, (jj + q) * 8 : (jj + q + 1) * 8, :] = piece.astype(BF)
    ninth = dot_nn(last, x)
    for jj in range(8):
        scr[pl.ds(jj, NE, stride=8), :] = ninth[:, jj * 128 : (jj + 1) * 128]
    out_ref[:, 64:72, :] = scr[...].reshape(NE, 8, 128).astype(BF)


def slot_tables(ids_ref):
    e_iota = lax.broadcasted_iota(jnp.int32, (NE, TOK), 0)
    named = jnp.zeros((NE, TOK), F32)
    for k in range(TOPK):
        named = named + jnp.where(ids_ref[k : k + 1, :] == e_iota, 1.0, 0.0)
    before = jnp.where(
        lax.broadcasted_iota(jnp.int32, (TOK, TOK), 0)
        < lax.broadcasted_iota(jnp.int32, (TOK, TOK), 1),
        1.0,
        0.0,
    ).astype(BF)
    count = dot_nn(named.astype(BF), before)
    return e_iota, jnp.where(named > 0.5, count, -1.0)


def spread_matrix():
    r = lax.broadcasted_iota(jnp.int32, (NE * 8, NE), 0)
    c = lax.broadcasted_iota(jnp.int32, (NE * 8, NE), 1)
    return jnp.where(lax.shift_right_logical(r, 3) == c, 1.0, 0.0).astype(BF)


def slot_number():
    r = lax.broadcasted_iota(jnp.int32, (NE * 8, TOK), 0)
    return jnp.bitwise_and(r, 7).astype(F32)


def route_pack_kernel(ids_ref, x_ref, pick_ref, out_ref, scr):
    @pl.when(pl.program_id(0) == 0)
    def _():
        _, count = slot_tables(ids_ref)
        wide = dot_nn(spread_matrix(), count.astype(BF))
        pick_ref[: NE * 8] = jnp.where(wide == slot_number(), 1.0, 0.0).astype(BF)
        pick_ref[NE * 8 :] = jnp.where(count == 8.0, 1.0, 0.0).astype(BF)

    pack_half(x_ref[...], pick_ref[...], out_ref, scr)


def route_pack(ids_t, x):
    return pl.pallas_call(
        route_pack_kernel,
        grid=(2,),
        in_specs=[
            pl.BlockSpec((TOPK, TOK), lambda n: (0, 0)),
            pl.BlockSpec((TOK, HALF), lambda n: (0, n)),
        ],
        out_specs=[
            pl.BlockSpec((NE * CAP, TOK), lambda n: (0, 0)),
            pl.BlockSpec((NE, MSG, 128), lambda n: (0, n, 0)),
        ],
        out_shape=[
            jax.ShapeDtypeStruct((NE * CAP, TOK), BF),
            jax.ShapeDtypeStruct((NE, 2 * MSG, 128), BF),
        ],
        scratch_shapes=[pltpu.VMEM((NE * 8, 128), F32)],
        compiler_params=params(1),
        name="route_pack",
    )(ids_t, x)


def weights_kernel(ids_ref, rw_ref, out_ref):
    e_iota, count = slot_tables(ids_ref)
    weight = jnp.zeros((NE, TOK), F32)
    for k in range(TOPK):
        weight = weight + jnp.where(ids_ref[k : k + 1, :] == e_iota, rw_ref[k : k + 1, :], 0.0)
    high = weight.astype(BF)
    low = (weight - high.astype(F32)).astype(BF)
    spread = spread_matrix()
    hit = dot_nn(spread, count.astype(BF)) == slot_number()
    for i, part in enumerate((high, low)):
        wide = jnp.where(hit, dot_nn(spread, part), 0.0)
        out_ref[i * TOK : (i + 1) * TOK, : NE * 8] = wide.T.astype(BF)
        tail = jnp.where(count == 8.0, part.astype(F32), 0.0)
        out_ref[i * TOK : (i + 1) * TOK, NE * 8 :] = tail.T.astype(BF)


def combine_weights(ids_t, rw_t):
    return pl.pallas_call(
        weights_kernel,
        out_shape=jax.ShapeDtypeStruct((2 * TOK, NE * CAP), BF),
        compiler_params=pltpu.CompilerParams(vmem_limit_bytes=VMEM_LIMIT),
        name="combine_weights",
    )(ids_t, rw_t)


def attention_kernel(kv_ref, q_ref, g_ref, k_ref, v_ref, out_ref, dk_acc, dv_acc):
    del kv_ref
    blk = 256
    factor = SCALE * math.log2(math.e)
    k_all = k_ref[...]
    k_t = k_all.astype(F32).T.astype(BF)
    allowed = lax.broadcasted_iota(jnp.int32, (blk, blk), 0) <= lax.broadcasted_iota(
        jnp.int32, (blk, blk), 1
    )
    first = True
    for h in range(2):
        for qb in reversed(range(DOC // blk)):
            length = (qb + 1) * blk
            q = q_ref[qb * blk : length, h * HD : (h + 1) * HD]
            g = g_ref[qb * blk : length, h * HD : (h + 1) * HD]
            k = k_ref[:length, :]
            v = v_ref[:length, :]
            s = dot_nt(k, q)
            diag = jnp.where(allowed, s[length - blk :], -jnp.inf)
            s = jnp.concatenate([s[: length - blk], diag], axis=0) if qb else diag
            top = jnp.max(s, axis=0, keepdims=True)
            expo = jnp.exp2((s - top) * factor)
            inv = 1.0 / jnp.sum(expo, axis=0, keepdims=True)
            dprob = dot_nt(v, g)
            delta = jnp.sum(expo * dprob, axis=0, keepdims=True) * inv
            probs = expo * inv
            dscore = (probs * (dprob - delta)).astype(BF)
            probs_b = probs.astype(BF)
            dq_t = dot_nn(k_t[:, :length], dscore) * SCALE
            dq = dq_t.T.astype(BF)
            y = (2 * qb) % N_Y
            z = qb // 2
            out_ref[y, z, :, h * HD : (h + 1) * HD] = dq[:128]
            out_ref[y + 1, z, :, h * HD : (h + 1) * HD] = dq[128:]
            dk = dot_nn(dscore, q)
            dv = dot_nn(probs_b, g)
            if first:
                dk_acc[...] = dk
                dv_acc[...] = dv
                first = False
            else:
                dk_acc[:length] += dk
                dv_acc[:length] += dv
    for b in range(DOC // 128):
        out_ref[b % N_Y, b // N_Y, :, 2 * HD : 3 * HD] = (
            dk_acc[b * 128 : (b + 1) * 128, :] * SCALE
        ).astype(BF)
        out_ref[b % N_Y, b // N_Y, :, 3 * HD :] = dv_acc[b * 128 : (b + 1) * 128, :].astype(BF)


def attention(kv_index, queries, out_grad, keys, values):
    docs = queries.shape[0] // DOC
    wide = pl.BlockSpec((DOC, 2 * HD), lambda d, kv: (d, 0))
    thin = pl.BlockSpec((DOC, HD), lambda d, kv: (d, kv[0]))
    return pl.pallas_call(
        attention_kernel,
        grid_spec=pltpu.PrefetchScalarGridSpec(
            num_scalar_prefetch=1,
            grid=(docs,),
            in_specs=[wide, wide, thin, thin],
            out_specs=pl.BlockSpec((N_Y, N_Z // docs, TOK, 4 * HD), lambda d, kv: (0, d, 0, 0)),
            scratch_shapes=[pltpu.VMEM((DOC, HD), F32), pltpu.VMEM((DOC, HD), F32)],
        ),
        out_shape=jax.ShapeDtypeStruct((N_Y, N_Z, TOK, 4 * HD), BF),
        compiler_params=params(1),
        name="attention",
    )(kv_index, queries, out_grad, keys, values)


def project_kernel(x_ref, wq_ref, wkv_ref, out_ref, kv_scr):
    @pl.when(pl.program_id(0) == 0)
    def _():
        total = x_ref[0, :, 2 * HD :].astype(F32)
        for y in range(1, N_Y):
            total = total + x_ref[y, :, 2 * HD :].astype(F32)
        kv_scr[...] = total.astype(BF)

    acc = dot_nt(kv_scr[...], wkv_ref[0])
    for y in range(N_Y):
        acc = acc + dot_nt(x_ref[y, :, : 2 * HD], wq_ref[y, 0])
    out_ref[...] = acc.astype(BF)


def project(x, wq, wkv):
    tokens = x.shape[1]
    cols, width = wq.shape[1], wq.shape[2]
    return pl.pallas_call(
        project_kernel,
        grid=(cols,),
        in_specs=[
            pl.BlockSpec((N_Y, tokens, 4 * HD), lambda n: (0, 0, 0)),
            pl.BlockSpec((N_Y, 1, width, 2 * HD), lambda n: (0, n, 0, 0)),
            pl.BlockSpec((1, width, 2 * HD), lambda n: (n, 0, 0)),
        ],
        out_specs=pl.BlockSpec((tokens, width), lambda n: (0, n)),
        out_shape=jax.ShapeDtypeStruct((tokens, cols * width), BF),
        scratch_shapes=[pltpu.VMEM((tokens, 2 * HD), BF)],
        compiler_params=params(1),
        name="project",
    )(x, wq, wkv)


def sum_pack_kernel(parts_ref, resid_ref, pick_ref, out_ref, scr):
    total = resid_ref[...].astype(F32)
    for z in range(N_Z):
        total = total + parts_ref[z].astype(F32)
    pack_half(total.astype(BF), pick_ref[...], out_ref, scr)


def sum_pack(parts, resid, pick):
    return pl.pallas_call(
        sum_pack_kernel,
        grid=(2,),
        in_specs=[
            pl.BlockSpec((N_Z, TOK, HALF), lambda n: (0, 0, n)),
            pl.BlockSpec((TOK, HALF), lambda n: (0, n)),
            pl.BlockSpec((NE * CAP, TOK), lambda n: (0, 0)),
        ],
        out_specs=pl.BlockSpec((NE, MSG, 128), lambda n: (0, n, 0)),
        out_shape=jax.ShapeDtypeStruct((NE, 2 * MSG, 128), BF),
        scratch_shapes=[pltpu.VMEM((NE * 8, 128), F32)],
        compiler_params=params(1),
        name="sum_pack",
    )(parts, resid, pick)


def unpack_rows(msg_ref, rows, scr):
    main = CHUNK * 8
    for n in range(2):
        scr[...] = msg_ref[:, n * MSG + 64 : (n + 1) * MSG, :].astype(F32).reshape(main, 128)
        for jj in range(8):
            at = (n * 8 + jj) * 128
            piece = msg_ref[:, n * MSG + jj * 8 : n * MSG + (jj + 1) * 8, :]
            rows[:main, at : at + 128] = piece.reshape(main, 128)
            rows[main:, at : at + 128] = scr[pl.ds(jj, CHUNK, stride=8), :].astype(BF)


def gate_up_kernel(msg_ref, w_ref, out_ref, rows, scr):
    unpack_rows(msg_ref, rows, scr)
    gate_up = dot_nn(rows[...], w_ref[...])
    gate = gate_up[:, :FF]
    up = gate_up[:, FF:]
    sigm = 1.0 / (1.0 + jnp.exp(-gate))
    out_ref[:, :FF] = up * sigm * (1.0 + gate * (1.0 - sigm))
    out_ref[:, FF:] = gate * sigm


def gate_factors(msg, w_gu):
    steps = NE // CHUNK
    return pl.pallas_call(
        gate_up_kernel,
        grid=(steps,),
        in_specs=[
            pl.BlockSpec((CHUNK, 2 * MSG, 128), lambda i: (i, 0, 0)),
            pl.BlockSpec((D, 2 * FF), lambda i: (0, 0)),
        ],
        out_specs=pl.BlockSpec((ROWS, 2 * FF), lambda i: (i, 0)),
        out_shape=jax.ShapeDtypeStruct((NE * CAP, 2 * FF), F32),
        scratch_shapes=[pltpu.VMEM((ROWS, D), BF), pltpu.VMEM((CHUNK * 8, 128), F32)],
        compiler_params=params(1),
        name="gate_factors",
    )(msg, w_gu)


def expert_kernel(msg_ref, fac_ref, wd_ref, w_ref, out_ref, rows, scr):
    main = CHUNK * 8
    unpack_rows(msg_ref, rows, scr)
    dhidden = dot_nt(rows[...], wd_ref[...])
    d_gate = (dhidden * fac_ref[:, :FF]).astype(BF)
    d_up = (dhidden * fac_ref[:, FF:]).astype(BF)
    both = jnp.concatenate([d_gate, d_up], axis=1)
    for n in range(2):
        back = dot_nt(both, w_ref[n * HALF : (n + 1) * HALF, :])
        for jj in range(8):
            piece = back[:main, jj * 128 : (jj + 1) * 128].reshape(CHUNK, 8, 128)
            out_ref[:, n * MSG + jj * 8 : n * MSG + (jj + 1) * 8, :] = piece.astype(BF)
            scr[pl.ds(jj, CHUNK, stride=8), :] = back[main:, jj * 128 : (jj + 1) * 128]
        out_ref[:, n * MSG + 64 : (n + 1) * MSG, :] = scr[...].reshape(CHUNK, 8, 128).astype(BF)


def expert_back(msg, factors, w_dn, w_gu):
    steps = NE // CHUNK
    return pl.pallas_call(
        expert_kernel,
        grid=(steps,),
        in_specs=[
            pl.BlockSpec((CHUNK, 2 * MSG, 128), lambda i: (i, 0, 0)),
            pl.BlockSpec((ROWS, 2 * FF), lambda i: (i, 0)),
            pl.BlockSpec((FF, D), lambda i: (0, 0)),
            pl.BlockSpec((D, 2 * FF), lambda i: (0, 0)),
        ],
        out_specs=pl.BlockSpec((CHUNK, 2 * MSG, 128), lambda i: (i, 0, 0)),
        out_shape=jax.ShapeDtypeStruct((NE, 2 * MSG, 128), BF),
        scratch_shapes=[pltpu.VMEM((ROWS, D), BF), pltpu.VMEM((CHUNK * 8, 128), F32)],
        compiler_params=params(1),
        name="expert_back",
    )(msg, factors, w_dn, w_gu)


def combine_kernel(msg_ref, w_ref, out_ref, scr):
    scr[...] = msg_ref[:, 64:72, :].astype(F32).reshape(NE * 8, 128)
    w_main = w_ref[:, : NE * 8]
    w_last = w_ref[:, NE * 8 :]
    for jj in range(8):
        piece = msg_ref[:, jj * 8 : (jj + 1) * 8, :].reshape(NE * 8, 128)
        ninth = scr[pl.ds(jj, NE, stride=8), :].astype(BF)
        both = dot_nn(w_main, piece) + dot_nn(w_last, ninth)
        out_ref[:, jj * 128 : (jj + 1) * 128] = (both[:TOK] + both[TOK:]).astype(BF)


def combine(msg, weights):
    return pl.pallas_call(
        combine_kernel,
        grid=(2,),
        in_specs=[
            pl.BlockSpec((NE, MSG, 128), lambda n: (0, n, 0)),
            pl.BlockSpec((2 * TOK, NE * CAP), lambda n: (0, 0)),
        ],
        out_specs=pl.BlockSpec((TOK, HALF), lambda n: (0, n)),
        out_shape=jax.ShapeDtypeStruct((TOK, D), BF),
        scratch_shapes=[pltpu.VMEM((NE * 8, 128), F32)],
        compiler_params=params(1),
        name="combine",
    )(msg, weights)


def exchange(x, axis, groups=None):
    return lax.all_to_all(
        x, axis, split_axis=0, concat_axis=0, tiled=True, axis_index_groups=groups
    )


def body(
    queries,
    keys,
    values,
    out_grad,
    q_weight,
    k_weight,
    v_weight,
    resid_grad,
    moe_input,
    expert_ids,
    route_weights,
    w_gate_up,
    w_down,
):
    n_col = lax.axis_size("col")
    row_of = [[N_Y * z + y for y in range(N_Y)] for z in range(N_Z)]
    same_y = [[N_Y * z + y for z in range(N_Z)] for y in range(N_Y)]
    planes = [[n_col * r + c for r in rows for c in range(n_col)] for rows in row_of]
    kv_index = lax.axis_index("row") // N_Y

    wk = lax.dynamic_slice_in_dim(k_weight, kv_index * HD, HD, 1)
    wv = lax.dynamic_slice_in_dim(v_weight, kv_index * HD, HD, 1)
    wq_all = lax.all_gather(
        q_weight, ("row", "col"), axis=0, tiled=True, axis_index_groups=planes
    ).reshape(N_Y, n_col, D // n_col, 2 * HD)
    wkv_all = lax.all_gather(
        jnp.concatenate([wk, wv], axis=1), "col", axis=0, tiled=True
    ).reshape(n_col, D // n_col, 2 * HD)

    ids_t = expert_ids.T
    pick, send_rows = route_pack(ids_t, moe_input)
    got_rows = exchange(send_rows, ALL)
    weights = combine_weights(ids_t, route_weights.T)

    dqkv = attention(kv_index.reshape(1).astype(jnp.int32), queries, out_grad, keys, values)
    dqkv = exchange(dqkv.reshape(N_Y, N_Z * TOK, 4 * HD), "row", row_of)
    term = project(dqkv, wq_all, wkv_all)
    parts = exchange(term.reshape(N_Z, TOK, D), "row", same_y)

    got_grads = exchange(sum_pack(parts, resid_grad, pick), ALL)
    w_gu = w_gate_up.reshape(D, 2 * FF)
    factors = gate_factors(got_rows, w_gu)
    back = expert_back(got_grads, factors, w_down.reshape(FF, D), w_gu)
    return combine(exchange(back, ALL), weights)


def solution(mesh):
    return jax.shard_map(
        body,
        mesh=mesh,
        in_specs=(
            P(("section", "col"), "row"),
            P(("section", "col"), None),
            P(("section", "col"), None),
            P(("section", "col"), "row"),
            P("col", "row"),
            P("col", None),
            P("col", None),
            P(ALL, None),
            P(ALL, None),
            P(ALL, None),
            P(ALL, None),
            P(ALL, None, None),
            P(ALL, None, None),
        ),
        out_specs=P(ALL, None),
        check_vma=False,
    )
```

```python
import math

import jax
import jax.numpy as jnp
from jax import lax
from jax.experimental import pallas as pl
from jax.experimental.pallas import tpu as pltpu
from jax.sharding import PartitionSpec as P

HEADS = 32
KV_HEADS = 4
HD = 128
TOPK = 8
DOC = 1024
D = 2048
FF = 768
CAP = 9
TOK = 128
NE = 128
N_Y = 4
N_Z = 4
HALF = 1024
MSG = 72
CHUNK = 32
ROWS = CHUNK * CAP
BF = jnp.bfloat16
F32 = jnp.float32
VMEM_LIMIT = 60 * 1024 * 1024
ALL = ("section", "row", "col")
SCALE = HD ** (-0.5)


def params(steps):
    return pltpu.CompilerParams(
        dimension_semantics=("arbitrary",) * steps, vmem_limit_bytes=VMEM_LIMIT
    )


def cost(us):
    return pl.CostEstimate(flops=int(us * 1.1e9), transcendentals=0, bytes_accessed=int(us * 3e6))


def dot_nn(a, b):
    return lax.dot_general(a, b, (((1,), (0,)), ((), ())), preferred_element_type=F32)


def dot_nt(a, b):
    return lax.dot_general(a, b, (((1,), (1,)), ((), ())), preferred_element_type=F32)


def pack_half(x, pick, out_ref, scr):
    main = pick[: NE * 8]
    last = pick[NE * 8 :]
    for jj in range(0, 8, 2):
        got = dot_nn(main, x[:, jj * 128 : (jj + 2) * 128])
        for q in range(2):
            piece = got[:, q * 128 : (q + 1) * 128].reshape(NE, 8, 128)
            out_ref[:, (jj + q) * 8 : (jj + q + 1) * 8, :] = piece.astype(BF)
    ninth = dot_nn(last, x)
    for jj in range(8):
        scr[pl.ds(jj, NE, stride=8), :] = ninth[:, jj * 128 : (jj + 1) * 128]
    out_ref[:, 64:72, :] = scr[...].reshape(NE, 8, 128).astype(BF)


def slot_tables(ids_ref):
    e_iota = lax.broadcasted_iota(jnp.int32, (NE, TOK), 0)
    named = jnp.zeros((NE, TOK), F32)
    for k in range(TOPK):
        named = named + jnp.where(ids_ref[k : k + 1, :] == e_iota, 1.0, 0.0)
    before = jnp.where(
        lax.broadcasted_iota(jnp.int32, (TOK, TOK), 0)
        < lax.broadcasted_iota(jnp.int32, (TOK, TOK), 1),
        1.0,
        0.0,
    ).astype(BF)
    count = dot_nn(named.astype(BF), before)
    return e_iota, jnp.where(named > 0.5, count, -1.0)


def spread_matrix():
    r = lax.broadcasted_iota(jnp.int32, (NE * 8, NE), 0)
    c = lax.broadcasted_iota(jnp.int32, (NE * 8, NE), 1)
    return jnp.where(lax.shift_right_logical(r, 3) == c, 1.0, 0.0).astype(BF)


def slot_number():
    r = lax.broadcasted_iota(jnp.int32, (NE * 8, TOK), 0)
    return jnp.bitwise_and(r, 7).astype(F32)


def route_pack_kernel(ids_ref, x_ref, pick_ref, out0, out1, scr):
    _, count = slot_tables(ids_ref)
    wide = dot_nn(spread_matrix(), count.astype(BF))
    pick_ref[: NE * 8] = jnp.where(wide == slot_number(), 1.0, 0.0).astype(BF)
    pick_ref[NE * 8 :] = jnp.where(count == 8.0, 1.0, 0.0).astype(BF)
    for n, out in enumerate((out0, out1)):
        pack_half(x_ref[:, n * HALF : (n + 1) * HALF], pick_ref[...], out, scr)


def route_pack(ids_t, x):
    half = jax.ShapeDtypeStruct((NE, MSG, 128), BF)
    return pl.pallas_call(
        route_pack_kernel,
        out_shape=[jax.ShapeDtypeStruct((NE * CAP, TOK), BF), half, half],
        scratch_shapes=[pltpu.VMEM((NE * 8, 128), F32)],
        compiler_params=pltpu.CompilerParams(vmem_limit_bytes=VMEM_LIMIT),
        name="route_pack",
        cost_estimate=cost(5),
    )(ids_t, x)


def weights_kernel(ids_ref, rw_ref, out_ref):
    e_iota, count = slot_tables(ids_ref)
    weight = jnp.zeros((NE, TOK), F32)
    for k in range(TOPK):
        weight = weight + jnp.where(ids_ref[k : k + 1, :] == e_iota, rw_ref[k : k + 1, :], 0.0)
    high = weight.astype(BF)
    low = (weight - high.astype(F32)).astype(BF)
    spread = spread_matrix()
    hit = dot_nn(spread, count.astype(BF)) == slot_number()
    for i, part in enumerate((high, low)):
        wide = jnp.where(hit, dot_nn(spread, part), 0.0)
        out_ref[i * TOK : (i + 1) * TOK, : NE * 8] = wide.T.astype(BF)
        tail = jnp.where(count == 8.0, part.astype(F32), 0.0)
        out_ref[i * TOK : (i + 1) * TOK, NE * 8 :] = tail.T.astype(BF)


def combine_weights(ids_t, rw_t):
    return pl.pallas_call(
        weights_kernel,
        out_shape=jax.ShapeDtypeStruct((2 * TOK, NE * CAP), BF),
        compiler_params=pltpu.CompilerParams(vmem_limit_bytes=VMEM_LIMIT),
        name="combine_weights",
        cost_estimate=cost(2.2),
    )(ids_t, rw_t)


def attention_kernel(
    at_ref, q_ref, g_ref, k_ref, v_ref, out0, out1, out2, out3, dk_acc, dv_acc, out_ref
):
    blk = 256
    factor = SCALE * math.log2(math.e)
    k_all = k_ref[...]
    k_t = k_all.astype(F32).T.astype(BF)
    allowed = lax.broadcasted_iota(jnp.int32, (blk, blk), 0) <= lax.broadcasted_iota(
        jnp.int32, (blk, blk), 1
    )
    first = True
    for h in range(2):
        for qb in reversed(range(DOC // blk)):
            length = (qb + 1) * blk
            q = q_ref[qb * blk : length, h * HD : (h + 1) * HD]
            g = g_ref[qb * blk : length, h * HD : (h + 1) * HD]
            k = k_ref[:length, :]
            v = v_ref[:length, :]
            s = dot_nt(k, q)
            diag = jnp.where(allowed, s[length - blk :], -jnp.inf)
            s = jnp.concatenate([s[: length - blk], diag], axis=0) if qb else diag
            top = jnp.max(s, axis=0, keepdims=True)
            expo = jnp.exp2((s - top) * factor)
            inv = 1.0 / jnp.sum(expo, axis=0, keepdims=True)
            dprob = dot_nt(v, g)
            delta = jnp.sum(expo * dprob, axis=0, keepdims=True) * inv
            probs = expo * inv
            dscore = (probs * (dprob - delta)).astype(BF)
            probs_b = probs.astype(BF)
            dq_t = dot_nn(k_t[:, :length], dscore) * SCALE
            dq = dq_t.T.astype(BF)
            y = (2 * qb) % N_Y
            z = qb // 2
            out_ref[y, z, :, h * HD : (h + 1) * HD] = dq[:128]
            out_ref[y + 1, z, :, h * HD : (h + 1) * HD] = dq[128:]
            dk = dot_nn(dscore, q)
            dv = dot_nn(probs_b, g)
            if first:
                dk_acc[...] = dk
                dv_acc[...] = dv
                first = False
            else:
                dk_acc[:length] += dk
                dv_acc[:length] += dv
    for b in range(DOC // 128):
        out_ref[b % N_Y, b // N_Y, :, 2 * HD : 3 * HD] = (
            dk_acc[b * 128 : (b + 1) * 128, :] * SCALE
        ).astype(BF)
        out_ref[b % N_Y, b // N_Y, :, 3 * HD :] = dv_acc[b * 128 : (b + 1) * 128, :].astype(BF)
    for k, out in enumerate((out0, out1, out2, out3)):
        out[...] = out_ref[jnp.bitwise_and(at_ref[1] + k, N_Y - 1)]


def attention(place, queries, out_grad, keys, values):
    docs = queries.shape[0] // DOC
    wide = pl.BlockSpec((DOC, 2 * HD), lambda d, at: (d, 0))
    thin = pl.BlockSpec((DOC, HD), lambda d, at: (d, at[0]))
    piece = pl.BlockSpec((N_Z // docs, TOK, 4 * HD), lambda d, at: (d, 0, 0))
    return pl.pallas_call(
        attention_kernel,
        grid_spec=pltpu.PrefetchScalarGridSpec(
            num_scalar_prefetch=1,
            grid=(docs,),
            in_specs=[wide, wide, thin, thin],
            out_specs=[piece] * N_Y,
            scratch_shapes=[
                pltpu.VMEM((DOC, HD), F32),
                pltpu.VMEM((DOC, HD), F32),
                pltpu.VMEM((N_Y, N_Z // docs, TOK, 4 * HD), BF),
            ],
        ),
        out_shape=[jax.ShapeDtypeStruct((N_Z, TOK, 4 * HD), BF)] * N_Y,
        compiler_params=params(1),
        name="attention",
        cost_estimate=cost(16),
    )(place, queries, out_grad, keys, values)


def project_kernel(at_ref, x0, x1, x2, x3, w0, w1, w2, w3, out0, out1, out2, out3, scr):
    pieces = (x0, x1, x2, x3)
    total = x0[:, 2 * HD :].astype(F32)
    for x in pieces[1:]:
        total = total + x[:, 2 * HD :].astype(F32)
    total = total.astype(BF)
    width = scr.shape[3]
    for k, w_ref in enumerate((w0, w1, w2, w3)):
        acc = dot_nt(total, w_ref[N_Y * width :])
        for y, x in enumerate(pieces):
            acc = acc + dot_nt(x[:, : 2 * HD], w_ref[y * width : (y + 1) * width])
        col = jnp.bitwise_and(at_ref[3] - k, 3)
        for z in range(N_Z):
            scr[z, col] = acc[z * TOK : (z + 1) * TOK].astype(BF)
    for k, out in enumerate((out0, out1, out2, out3)):
        out[...] = scr[jnp.bitwise_and(at_ref[0] + k, N_Z - 1)]


def project(place, pieces, weights):
    width = weights[0].shape[0] // (N_Y + 1)
    out = jax.ShapeDtypeStruct((len(weights), TOK, width), BF)
    whole = pl.BlockSpec(memory_space=pltpu.VMEM)
    return pl.pallas_call(
        project_kernel,
        in_specs=[pl.BlockSpec(memory_space=pltpu.SMEM)] + [whole] * 8,
        out_specs=[whole] * N_Z,
        out_shape=[out] * N_Z,
        scratch_shapes=[pltpu.VMEM((N_Z, len(weights), TOK, width), BF)],
        compiler_params=pltpu.CompilerParams(vmem_limit_bytes=VMEM_LIMIT),
        name="project",
        cost_estimate=cost(6),
    )(place, *pieces, *weights)


def sum_pack_kernel(at_ref, m0, m1, m2, m3, o0, o1, o2, o3, resid_ref, pick_ref, out_ref, scr):
    blocks = []
    for c in range(2):
        mine, other = (
            sum((x[c].astype(F32) for x in xs[1:]), xs[0][c].astype(F32))
            for xs in ((m0, m1, m2, m3), (o0, o1, o2, o3))
        )
        for h in range(2):
            blocks.append(jnp.where(at_ref[2] == h, mine, other))
    total = resid_ref[...].astype(F32) + jnp.concatenate(blocks, axis=1)
    pack_half(total.astype(BF), pick_ref[...], out_ref, scr)


def sum_pack(place, mine, other, resid, pick):
    part = pl.BlockSpec((2, TOK, 256), lambda n, at: (n, 0, 0))
    return pl.pallas_call(
        sum_pack_kernel,
        grid_spec=pltpu.PrefetchScalarGridSpec(
            num_scalar_prefetch=1,
            grid=(2,),
            in_specs=[part] * 8
            + [
                pl.BlockSpec((TOK, HALF), lambda n, at: (0, n)),
                pl.BlockSpec((NE * CAP, TOK), lambda n, at: (0, 0)),
            ],
            out_specs=pl.BlockSpec((NE, MSG, 128), lambda n, at: (0, n, 0)),
            scratch_shapes=[pltpu.VMEM((NE * 8, 128), F32)],
        ),
        out_shape=jax.ShapeDtypeStruct((NE, 2 * MSG, 128), BF),
        compiler_params=params(1),
        name="sum_pack",
        cost_estimate=cost(5.5),
    )(place, *mine, *other, resid, pick)


def unpack_rows(halves, rows, scr):
    main = CHUNK * 8
    for n, msg_ref in enumerate(halves):
        scr[...] = msg_ref[:, 64:, :].astype(F32).reshape(main, 128)
        for jj in range(8):
            at = (n * 8 + jj) * 128
            piece = msg_ref[:, jj * 8 : (jj + 1) * 8, :]
            rows[:main, at : at + 128] = piece.reshape(main, 128)
            rows[main:, at : at + 128] = scr[pl.ds(jj, CHUNK, stride=8), :].astype(BF)


def gate_up_kernel(msg0, msg1, w_ref, out_ref, rows, scr):
    unpack_rows((msg0, msg1), rows, scr)
    gate_up = dot_nn(rows[...], w_ref[...])
    gate = gate_up[:, :FF]
    up = gate_up[:, FF:]
    sigm = 1.0 / (1.0 + jnp.exp(-gate))
    out_ref[:, :FF] = (up * sigm * (1.0 + gate * (1.0 - sigm))).astype(BF)
    out_ref[:, FF:] = (gate * sigm).astype(BF)


def gate_factors(halves, w_gu):
    steps = NE // CHUNK
    return pl.pallas_call(
        gate_up_kernel,
        grid=(steps,),
        in_specs=[
            pl.BlockSpec((CHUNK, MSG, 128), lambda i: (i, 0, 0)),
            pl.BlockSpec((CHUNK, MSG, 128), lambda i: (i, 0, 0)),
            pl.BlockSpec((D, 2 * FF), lambda i: (0, 0)),
        ],
        out_specs=pl.BlockSpec((ROWS, 2 * FF), lambda i: (i, 0)),
        out_shape=jax.ShapeDtypeStruct((NE * CAP, 2 * FF), BF),
        scratch_shapes=[pltpu.VMEM((ROWS, D), BF), pltpu.VMEM((CHUNK * 8, 128), F32)],
        compiler_params=params(1),
        name="gate_factors",
        cost_estimate=cost(12.5),
    )(*halves, w_gu)


def expert_kernel(msg0, msg1, fac_ref, wd_ref, w_ref, out_ref, rows, scr):
    main = CHUNK * 8
    unpack_rows((msg0, msg1), rows, scr)
    dhidden = dot_nt(rows[...], wd_ref[...])
    d_gate = (dhidden * fac_ref[:, :FF].astype(F32)).astype(BF)
    d_up = (dhidden * fac_ref[:, FF:].astype(F32)).astype(BF)
    both = jnp.concatenate([d_gate, d_up], axis=1)
    for n in range(2):
        back = dot_nt(both, w_ref[n * HALF : (n + 1) * HALF, :])
        for jj in range(8):
            piece = back[:main, jj * 128 : (jj + 1) * 128].reshape(CHUNK, 8, 128)
            out_ref[:, n * MSG + jj * 8 : n * MSG + (jj + 1) * 8, :] = piece.astype(BF)
            scr[pl.ds(jj, CHUNK, stride=8), :] = back[main:, jj * 128 : (jj + 1) * 128]
        out_ref[:, n * MSG + 64 : (n + 1) * MSG, :] = scr[...].reshape(CHUNK, 8, 128).astype(BF)


def expert_back(msg, factors, w_dn, w_gu):
    steps = NE // CHUNK
    return pl.pallas_call(
        expert_kernel,
        grid=(steps,),
        in_specs=[
            pl.BlockSpec((CHUNK, MSG, 128), lambda i: (i, 0, 0)),
            pl.BlockSpec((CHUNK, MSG, 128), lambda i: (i, 1, 0)),
            pl.BlockSpec((ROWS, 2 * FF), lambda i: (i, 0)),
            pl.BlockSpec((FF, D), lambda i: (0, 0)),
            pl.BlockSpec((D, 2 * FF), lambda i: (0, 0)),
        ],
        out_specs=pl.BlockSpec((CHUNK, 2 * MSG, 128), lambda i: (i, 0, 0)),
        out_shape=jax.ShapeDtypeStruct((NE, 2 * MSG, 128), BF),
        scratch_shapes=[pltpu.VMEM((ROWS, D), BF), pltpu.VMEM((CHUNK * 8, 128), F32)],
        compiler_params=params(1),
        name="expert_back",
        cost_estimate=cost(20),
    )(msg, msg, factors, w_dn, w_gu)


def combine_kernel(msg_ref, w_ref, out_ref, scr):
    scr[...] = msg_ref[:, 64:72, :].astype(F32).reshape(NE * 8, 128)
    w_main = w_ref[:, : NE * 8]
    w_last = w_ref[:, NE * 8 :]
    for jj in range(8):
        piece = msg_ref[:, jj * 8 : (jj + 1) * 8, :].reshape(NE * 8, 128)
        ninth = scr[pl.ds(jj, NE, stride=8), :].astype(BF)
        both = dot_nn(w_main, piece) + dot_nn(w_last, ninth)
        out_ref[:, jj * 128 : (jj + 1) * 128] = (both[:TOK] + both[TOK:]).astype(BF)


def combine(msg, weights):
    return pl.pallas_call(
        combine_kernel,
        grid=(2,),
        in_specs=[
            pl.BlockSpec((NE, MSG, 128), lambda n: (0, n, 0)),
            pl.BlockSpec((2 * TOK, NE * CAP), lambda n: (0, 0)),
        ],
        out_specs=pl.BlockSpec((TOK, HALF), lambda n: (0, n)),
        out_shape=jax.ShapeDtypeStruct((TOK, D), BF),
        scratch_shapes=[pltpu.VMEM((NE * 8, 128), F32)],
        compiler_params=params(1),
        name="combine",
        cost_estimate=cost(5.3),
    )(msg, weights)


def exchange(x, axis, groups=None):
    return lax.all_to_all(
        x, axis, split_axis=0, concat_axis=0, tiled=True, axis_index_groups=groups
    )


def body(
    queries,
    keys,
    values,
    out_grad,
    q_weight,
    k_weight,
    v_weight,
    resid_grad,
    moe_input,
    expert_ids,
    route_weights,
    w_gate_up,
    w_down,
):
    n_col = lax.axis_size("col")
    row = lax.axis_index("row")
    kv_index = row // N_Y
    section = lax.axis_index("section")
    place = jnp.stack([kv_index, row % N_Y, section, lax.axis_index("col")]).astype(jnp.int32)
    others = range(1, N_Y)

    def ahead_y(x, k):
        hops = [(N_Y * z + y, N_Y * z + (y + k) % N_Y) for z in range(N_Z) for y in range(N_Y)]
        return lax.ppermute(x, "row", hops)

    def ahead_z(x, k):
        hops = [(N_Y * z + y, N_Y * ((z + k) % N_Z) + y) for z in range(N_Z) for y in range(N_Y)]
        return lax.ppermute(x, "row", hops)

    def ahead_c(x, k):
        return lax.ppermute(x, "col", [(c, (c + k) % n_col) for c in range(n_col)])

    half = D // n_col // 2
    wq = lax.dynamic_slice_in_dim(q_weight, section * half, half, 0)
    wk = lax.dynamic_slice(k_weight, (section * half, kv_index * HD), (half, HD))
    wv = lax.dynamic_slice(v_weight, (section * half, kv_index * HD), (half, HD))
    w_own = jnp.concatenate(
        [wq, *(ahead_y(wq, k) for k in others), jnp.concatenate([wk, wv], axis=1)], axis=0
    )
    w_mine = [w_own] + [ahead_c(w_own, k) for k in others]
    w_other = [lax.ppermute(w, "section", [(0, 1), (1, 0)]) for w in w_mine]

    ids_t = expert_ids.T
    pick, *send_rows = route_pack(ids_t, moe_input)
    got_rows = [exchange(half_rows, ALL) for half_rows in send_rows]
    weights = combine_weights(ids_t, route_weights.T)

    queries, _ = lax.optimization_barrier((queries, pick))
    pieces = attention(place, queries, out_grad, keys, values)
    pieces = [p.reshape(N_Z * TOK, 4 * HD) for p in pieces]
    pieces = [pieces[0]] + [ahead_y(pieces[k], k) for k in others]

    def head_half(weights):
        parts = project(place, pieces, weights)
        return [parts[0]] + [ahead_z(parts[k], k) for k in others]

    head_mine = head_half(w_mine)
    head_other = head_half(w_other)
    got_grads = exchange(sum_pack(place, head_mine, head_other, resid_grad, pick), ALL)
    w_gu = w_gate_up.reshape(D, 2 * FF)
    factors = gate_factors(got_rows, w_gu)
    back = expert_back(got_grads, factors, w_down.reshape(FF, D), w_gu)
    return combine(exchange(back, ALL), weights)


def solution(mesh):
    return jax.shard_map(
        body,
        mesh=mesh,
        in_specs=(
            P(("section", "col"), "row"),
            P(("section", "col"), None),
            P(("section", "col"), None),
            P(("section", "col"), "row"),
            P("col", "row"),
            P("col", None),
            P("col", None),
            P(ALL, None),
            P(ALL, None),
            P(ALL, None),
            P(ALL, None),
            P(ALL, None, None),
            P(ALL, None, None),
        ),
        out_specs=P(ALL, None),
        check_vma=False,
    )
```

```python
import math

import jax
import jax.numpy as jnp
from jax import lax
from jax.experimental import pallas as pl
from jax.experimental.pallas import tpu as pltpu
from jax.sharding import PartitionSpec as P

HEADS = 32
KV_HEADS = 4
HD = 128
TOPK = 8
DOC = 1024
D = 2048
FF = 768
CAP = 9
TOK = 128
NE = 128
N_Y = 4
N_Z = 4
HALF = 1024
MSG = 72
CHUNK = 32
ROWS = CHUNK * CAP
BF = jnp.bfloat16
F32 = jnp.float32
VMEM_LIMIT = 60 * 1024 * 1024
ALL = ("section", "row", "col")
SCALE = HD ** (-0.5)


def params(steps):
    return pltpu.CompilerParams(
        dimension_semantics=("arbitrary",) * steps, vmem_limit_bytes=VMEM_LIMIT
    )


def cost(us):
    return pl.CostEstimate(flops=int(us * 1.1e9), transcendentals=0, bytes_accessed=int(us * 3e6))


def dot_nn(a, b):
    return lax.dot_general(a, b, (((1,), (0,)), ((), ())), preferred_element_type=F32)


def dot_nt(a, b):
    return lax.dot_general(a, b, (((1,), (1,)), ((), ())), preferred_element_type=F32)


def pack_half(x, pick, out_ref, scr):
    main = pick[: NE * 8]
    last = pick[NE * 8 :]
    for jj in range(0, 8, 2):
        got = dot_nn(main, x[:, jj * 128 : (jj + 2) * 128])
        for q in range(2):
            piece = got[:, q * 128 : (q + 1) * 128].reshape(NE, 8, 128)
            out_ref[:, (jj + q) * 8 : (jj + q + 1) * 8, :] = piece.astype(BF)
    ninth = dot_nn(last, x)
    for jj in range(8):
        scr[pl.ds(jj, NE, stride=8), :] = ninth[:, jj * 128 : (jj + 1) * 128]
    out_ref[:, 64:72, :] = scr[...].reshape(NE, 8, 128).astype(BF)


def slot_tables(ids_ref):
    e_iota = lax.broadcasted_iota(jnp.int32, (NE, TOK), 0)
    named = jnp.zeros((NE, TOK), F32)
    for k in range(TOPK):
        named = named + jnp.where(ids_ref[k : k + 1, :] == e_iota, 1.0, 0.0)
    before = jnp.where(
        lax.broadcasted_iota(jnp.int32, (TOK, TOK), 0)
        < lax.broadcasted_iota(jnp.int32, (TOK, TOK), 1),
        1.0,
        0.0,
    ).astype(BF)
    count = dot_nn(named.astype(BF), before)
    return e_iota, jnp.where(named > 0.5, count, -1.0)


def spread_matrix():
    r = lax.broadcasted_iota(jnp.int32, (NE * 8, NE), 0)
    c = lax.broadcasted_iota(jnp.int32, (NE * 8, NE), 1)
    return jnp.where(lax.shift_right_logical(r, 3) == c, 1.0, 0.0).astype(BF)


def slot_number():
    r = lax.broadcasted_iota(jnp.int32, (NE * 8, TOK), 0)
    return jnp.bitwise_and(r, 7).astype(F32)


def route_pack_kernel(ids_ref, x_ref, pick_ref, out0, out1, scr):
    _, count = slot_tables(ids_ref)
    wide = dot_nn(spread_matrix(), count.astype(BF))
    pick_ref[: NE * 8] = jnp.where(wide == slot_number(), 1.0, 0.0).astype(BF)
    pick_ref[NE * 8 :] = jnp.where(count == 8.0, 1.0, 0.0).astype(BF)
    for n, out in enumerate((out0, out1)):
        pack_half(x_ref[:, n * HALF : (n + 1) * HALF], pick_ref[...], out, scr)


def route_pack(ids_t, x):
    half = jax.ShapeDtypeStruct((NE, MSG, 128), BF)
    return pl.pallas_call(
        route_pack_kernel,
        out_shape=[jax.ShapeDtypeStruct((NE * CAP, TOK), BF), half, half],
        scratch_shapes=[pltpu.VMEM((NE * 8, 128), F32)],
        compiler_params=pltpu.CompilerParams(vmem_limit_bytes=VMEM_LIMIT),
        name="route_pack",
        cost_estimate=cost(5),
    )(ids_t, x)


def weights_kernel(ids_ref, rw_ref, out_ref):
    e_iota, count = slot_tables(ids_ref)
    weight = jnp.zeros((NE, TOK), F32)
    for k in range(TOPK):
        weight = weight + jnp.where(ids_ref[k : k + 1, :] == e_iota, rw_ref[k : k + 1, :], 0.0)
    high = weight.astype(BF)
    low = (weight - high.astype(F32)).astype(BF)
    spread = spread_matrix()
    hit = dot_nn(spread, count.astype(BF)) == slot_number()
    for i, part in enumerate((high, low)):
        wide = jnp.where(hit, dot_nn(spread, part), 0.0)
        out_ref[i * TOK : (i + 1) * TOK, : NE * 8] = wide.T.astype(BF)
        tail = jnp.where(count == 8.0, part.astype(F32), 0.0)
        out_ref[i * TOK : (i + 1) * TOK, NE * 8 :] = tail.T.astype(BF)


def combine_weights(ids_t, rw_t):
    return pl.pallas_call(
        weights_kernel,
        out_shape=jax.ShapeDtypeStruct((2 * TOK, NE * CAP), BF),
        compiler_params=pltpu.CompilerParams(vmem_limit_bytes=VMEM_LIMIT),
        name="combine_weights",
        cost_estimate=cost(2.2),
    )(ids_t, rw_t)


def attention_kernel(
    at_ref, q_ref, g_ref, k_ref, v_ref, out0, out1, out2, out3, dk_acc, dv_acc, out_ref
):
    blk = 256
    factor = SCALE * math.log2(math.e)
    k_all = k_ref[...]
    k_t = k_all.astype(F32).T.astype(BF)
    allowed = lax.broadcasted_iota(jnp.int32, (blk, blk), 0) <= lax.broadcasted_iota(
        jnp.int32, (blk, blk), 1
    )
    first = True
    for h in range(2):
        for qb in reversed(range(DOC // blk)):
            length = (qb + 1) * blk
            q = q_ref[qb * blk : length, h * HD : (h + 1) * HD]
            g = g_ref[qb * blk : length, h * HD : (h + 1) * HD]
            k = k_ref[:length, :]
            v = v_ref[:length, :]
            s = dot_nt(k, q)
            diag = jnp.where(allowed, s[length - blk :], -jnp.inf)
            s = jnp.concatenate([s[: length - blk], diag], axis=0) if qb else diag
            top = jnp.max(s, axis=0, keepdims=True)
            expo = jnp.exp2((s - top) * factor)
            inv = 1.0 / jnp.sum(expo, axis=0, keepdims=True)
            dprob = dot_nt(v, g)
            delta = jnp.sum(expo * dprob, axis=0, keepdims=True) * inv
            probs = expo * inv
            dscore = (probs * (dprob - delta)).astype(BF)
            probs_b = probs.astype(BF)
            dq_t = dot_nn(k_t[:, :length], dscore) * SCALE
            dq = dq_t.T.astype(BF)
            y = (2 * qb) % N_Y
            z = qb // 2
            out_ref[y, z, :, h * HD : (h + 1) * HD] = dq[:128]
            out_ref[y + 1, z, :, h * HD : (h + 1) * HD] = dq[128:]
            dk = dot_nn(dscore, q)
            dv = dot_nn(probs_b, g)
            if first:
                dk_acc[...] = dk
                dv_acc[...] = dv
                first = False
            else:
                dk_acc[:length] += dk
                dv_acc[:length] += dv
    for b in range(DOC // 128):
        out_ref[b % N_Y, b // N_Y, :, 2 * HD : 3 * HD] = (
            dk_acc[b * 128 : (b + 1) * 128, :] * SCALE
        ).astype(BF)
        out_ref[b % N_Y, b // N_Y, :, 3 * HD :] = dv_acc[b * 128 : (b + 1) * 128, :].astype(BF)
    for k, out in enumerate((out0, out1, out2, out3)):
        out[...] = out_ref[jnp.bitwise_and(at_ref[1] + k, N_Y - 1)]


def attention(place, queries, out_grad, keys, values):
    docs = queries.shape[0] // DOC
    wide = pl.BlockSpec((DOC, 2 * HD), lambda d, at: (d, 0))
    thin = pl.BlockSpec((DOC, HD), lambda d, at: (d, at[0]))
    piece = pl.BlockSpec((N_Z // docs, TOK, 4 * HD), lambda d, at: (d, 0, 0))
    return pl.pallas_call(
        attention_kernel,
        grid_spec=pltpu.PrefetchScalarGridSpec(
            num_scalar_prefetch=1,
            grid=(docs,),
            in_specs=[wide, wide, thin, thin],
            out_specs=[piece] * N_Y,
            scratch_shapes=[
                pltpu.VMEM((DOC, HD), F32),
                pltpu.VMEM((DOC, HD), F32),
                pltpu.VMEM((N_Y, N_Z // docs, TOK, 4 * HD), BF),
            ],
        ),
        out_shape=[jax.ShapeDtypeStruct((N_Z, TOK, 4 * HD), BF)] * N_Y,
        compiler_params=params(1),
        name="attention",
        cost_estimate=cost(16),
    )(place, queries, out_grad, keys, values)


def project_kernel(at_ref, x0, x1, x2, x3, *refs):
    *weights, out0, out1, out2, out3, scr = refs
    pieces = (x0, x1, x2, x3)
    total = x0[:, 2 * HD :].astype(F32)
    for x in pieces[1:]:
        total = total + x[:, 2 * HD :].astype(F32)
    total = total.astype(BF)
    width = scr.shape[3]
    unit = 0
    for w_ref in weights:
        for h in range(w_ref.shape[0]):
            acc = dot_nt(total, w_ref[h, N_Y * width :])
            for y, x in enumerate(pieces):
                acc = acc + dot_nt(x[:, : 2 * HD], w_ref[h, y * width : (y + 1) * width])
            for z in range(N_Z):
                scr[z, unit] = acc[z * TOK : (z + 1) * TOK].astype(BF)
            unit += 1
    for k, out in enumerate((out0, out1, out2, out3)):
        out[...] = scr[jnp.bitwise_and(at_ref[0] + k, N_Z - 1)]


def project(place, pieces, weights):
    width = weights[0].shape[1] // (N_Y + 1)
    units = sum(w.shape[0] for w in weights)
    whole = pl.BlockSpec(memory_space=pltpu.VMEM)
    return pl.pallas_call(
        project_kernel,
        in_specs=[pl.BlockSpec(memory_space=pltpu.SMEM)] + [whole] * (N_Y + len(weights)),
        out_specs=[whole] * N_Z,
        out_shape=[jax.ShapeDtypeStruct((units, TOK, width), BF)] * N_Z,
        scratch_shapes=[pltpu.VMEM((N_Z, units, TOK, width), BF)],
        compiler_params=pltpu.CompilerParams(vmem_limit_bytes=VMEM_LIMIT),
        name="project",
        cost_estimate=cost(0.6 * units),
    )(place, *pieces, *weights)


def sum_pack_kernel(at_ref, m0, m1, m2, m3, o0, o1, o2, o3, resid_ref, pick_ref, out_ref, sums, scr):
    @pl.when(pl.program_id(0) == 0)
    def _():
        mine = m0.shape[0]
        for u in range(mine):
            sums[u] = sum((x[u].astype(F32) for x in (m1, m2, m3)), m0[u].astype(F32))
        for u in range(o0.shape[0]):
            sums[mine + u] = sum((x[u].astype(F32) for x in (o1, o2, o3)), o0[u].astype(F32))

    section, col = at_ref[2], at_ref[3]
    blocks = []
    for c in range(2):
        behind = jnp.bitwise_and(2 * pl.program_id(0) + c - col, 3)
        for h in range(2):
            far = jnp.where(section == h, 4, 7)
            near = jnp.where(behind == jnp.where(section == 0, 3, 1), 2 + h, 5 + h)
            unit = jnp.where(behind == 0, h, jnp.where(behind == 2, far, near))
            blocks.append(sums[unit])
    total = resid_ref[...].astype(F32) + jnp.concatenate(blocks, axis=1)
    pack_half(total.astype(BF), pick_ref[...], out_ref, scr)


def sum_pack(place, mine, other, resid, pick):
    def whole(x):
        return pl.BlockSpec(x.shape, lambda n, at: (0, 0, 0))

    units = mine[0].shape[0] + other[0].shape[0]
    return pl.pallas_call(
        sum_pack_kernel,
        grid_spec=pltpu.PrefetchScalarGridSpec(
            num_scalar_prefetch=1,
            grid=(2,),
            in_specs=[whole(x) for x in (*mine, *other)]
            + [
                pl.BlockSpec((TOK, HALF), lambda n, at: (0, n)),
                pl.BlockSpec((NE * CAP, TOK), lambda n, at: (0, 0)),
            ],
            out_specs=pl.BlockSpec((NE, MSG, 128), lambda n, at: (0, n, 0)),
            scratch_shapes=[
                pltpu.VMEM((units, TOK, 256), F32),
                pltpu.VMEM((NE * 8, 128), F32),
            ],
        ),
        out_shape=jax.ShapeDtypeStruct((NE, 2 * MSG, 128), BF),
        compiler_params=params(1),
        name="sum_pack",
        cost_estimate=cost(4),
    )(place, *mine, *other, resid, pick)


def unpack_rows(halves, rows, scr):
    main = CHUNK * 8
    for n, msg_ref in enumerate(halves):
        scr[...] = msg_ref[:, 64:, :].astype(F32).reshape(main, 128)
        for jj in range(8):
            at = (n * 8 + jj) * 128
            piece = msg_ref[:, jj * 8 : (jj + 1) * 8, :]
            rows[:main, at : at + 128] = piece.reshape(main, 128)
            rows[main:, at : at + 128] = scr[pl.ds(jj, CHUNK, stride=8), :].astype(BF)


def gate_up_kernel(msg0, msg1, w_ref, out_ref, rows, scr):
    unpack_rows((msg0, msg1), rows, scr)
    gate_up = dot_nn(rows[...], w_ref[...])
    gate = gate_up[:, :FF]
    up = gate_up[:, FF:]
    sigm = 1.0 / (1.0 + jnp.exp(-gate))
    out_ref[:, :FF] = (up * sigm * (1.0 + gate * (1.0 - sigm))).astype(BF)
    out_ref[:, FF:] = (gate * sigm).astype(BF)


def gate_factors(halves, w_gu):
    steps = NE // CHUNK
    return pl.pallas_call(
        gate_up_kernel,
        grid=(steps,),
        in_specs=[
            pl.BlockSpec((CHUNK, MSG, 128), lambda i: (i, 0, 0)),
            pl.BlockSpec((CHUNK, MSG, 128), lambda i: (i, 0, 0)),
            pl.BlockSpec((D, 2 * FF), lambda i: (0, 0)),
        ],
        out_specs=pl.BlockSpec((ROWS, 2 * FF), lambda i: (i, 0)),
        out_shape=jax.ShapeDtypeStruct((NE * CAP, 2 * FF), BF),
        scratch_shapes=[pltpu.VMEM((ROWS, D), BF), pltpu.VMEM((CHUNK * 8, 128), F32)],
        compiler_params=params(1),
        name="gate_factors",
        cost_estimate=cost(12.5),
    )(*halves, w_gu)


def expert_kernel(msg0, msg1, fac_ref, wd_ref, w_ref, out_ref, rows, scr):
    main = CHUNK * 8
    unpack_rows((msg0, msg1), rows, scr)
    dhidden = dot_nt(rows[...], wd_ref[...])
    d_gate = (dhidden * fac_ref[:, :FF].astype(F32)).astype(BF)
    d_up = (dhidden * fac_ref[:, FF:].astype(F32)).astype(BF)
    both = jnp.concatenate([d_gate, d_up], axis=1)
    for n in range(2):
        back = dot_nt(both, w_ref[n * HALF : (n + 1) * HALF, :])
        for jj in range(8):
            piece = back[:main, jj * 128 : (jj + 1) * 128].reshape(CHUNK, 8, 128)
            out_ref[:, n * MSG + jj * 8 : n * MSG + (jj + 1) * 8, :] = piece.astype(BF)
            scr[pl.ds(jj, CHUNK, stride=8), :] = back[main:, jj * 128 : (jj + 1) * 128]
        out_ref[:, n * MSG + 64 : (n + 1) * MSG, :] = scr[...].reshape(CHUNK, 8, 128).astype(BF)


def expert_back(msg, factors, w_dn, w_gu):
    steps = NE // CHUNK
    return pl.pallas_call(
        expert_kernel,
        grid=(steps,),
        in_specs=[
            pl.BlockSpec((CHUNK, MSG, 128), lambda i: (i, 0, 0)),
            pl.BlockSpec((CHUNK, MSG, 128), lambda i: (i, 1, 0)),
            pl.BlockSpec((ROWS, 2 * FF), lambda i: (i, 0)),
            pl.BlockSpec((FF, D), lambda i: (0, 0)),
            pl.BlockSpec((D, 2 * FF), lambda i: (0, 0)),
        ],
        out_specs=pl.BlockSpec((CHUNK, 2 * MSG, 128), lambda i: (i, 0, 0)),
        out_shape=jax.ShapeDtypeStruct((NE, 2 * MSG, 128), BF),
        scratch_shapes=[pltpu.VMEM((ROWS, D), BF), pltpu.VMEM((CHUNK * 8, 128), F32)],
        compiler_params=params(1),
        name="expert_back",
        cost_estimate=cost(20),
    )(msg, msg, factors, w_dn, w_gu)


def combine_kernel(msg_ref, w_ref, out_ref, scr):
    scr[...] = msg_ref[:, 64:72, :].astype(F32).reshape(NE * 8, 128)
    w_main = w_ref[:, : NE * 8]
    w_last = w_ref[:, NE * 8 :]
    for jj in range(8):
        piece = msg_ref[:, jj * 8 : (jj + 1) * 8, :].reshape(NE * 8, 128)
        ninth = scr[pl.ds(jj, NE, stride=8), :].astype(BF)
        both = dot_nn(w_main, piece) + dot_nn(w_last, ninth)
        out_ref[:, jj * 128 : (jj + 1) * 128] = (both[:TOK] + both[TOK:]).astype(BF)


def combine(msg, weights):
    return pl.pallas_call(
        combine_kernel,
        grid=(2,),
        in_specs=[
            pl.BlockSpec((NE, MSG, 128), lambda n: (0, n, 0)),
            pl.BlockSpec((2 * TOK, NE * CAP), lambda n: (0, 0)),
        ],
        out_specs=pl.BlockSpec((TOK, HALF), lambda n: (0, n)),
        out_shape=jax.ShapeDtypeStruct((TOK, D), BF),
        scratch_shapes=[pltpu.VMEM((NE * 8, 128), F32)],
        compiler_params=params(1),
        name="combine",
        cost_estimate=cost(5.3),
    )(msg, weights)


def exchange(x, axis, groups=None):
    return lax.all_to_all(
        x, axis, split_axis=0, concat_axis=0, tiled=True, axis_index_groups=groups
    )


def body(
    queries,
    keys,
    values,
    out_grad,
    q_weight,
    k_weight,
    v_weight,
    resid_grad,
    moe_input,
    expert_ids,
    route_weights,
    w_gate_up,
    w_down,
):
    n_col = lax.axis_size("col")
    row = lax.axis_index("row")
    kv_index = row // N_Y
    section = lax.axis_index("section")
    place = jnp.stack([kv_index, row % N_Y, section, lax.axis_index("col")]).astype(jnp.int32)
    others = range(1, N_Y)

    def ahead_y(x, k):
        hops = [(N_Y * z + y, N_Y * z + (y + k) % N_Y) for z in range(N_Z) for y in range(N_Y)]
        return lax.ppermute(x, "row", hops)

    def ahead_z(x, k):
        hops = [(N_Y * z + y, N_Y * ((z + k) % N_Z) + y) for z in range(N_Z) for y in range(N_Y)]
        return lax.ppermute(x, "row", hops)

    half = D // n_col // 2
    wk = lax.dynamic_slice_in_dim(k_weight, kv_index * HD, HD, 1)
    wv = lax.dynamic_slice_in_dim(v_weight, kv_index * HD, HD, 1)
    w_own = jnp.concatenate(
        [
            w.reshape(2, half, 2 * HD)
            for w in (
                q_weight,
                *(ahead_y(q_weight, k) for k in others),
                jnp.concatenate([wk, wv], axis=1),
            )
        ],
        axis=1,
    )
    near_hops = [(c, (c + 1) % n_col) for c in range(n_col)]
    near_hops += [(n_col + c, n_col + (c - 1) % n_col) for c in range(n_col)]
    w_near = lax.ppermute(w_own, ("section", "col"), near_hops)
    w_far = lax.ppermute(
        lax.dynamic_slice_in_dim(w_own, section, 1, 0),
        "col",
        [(c, (c + 2) % n_col) for c in range(n_col)],
    )

    ids_t = expert_ids.T
    pick, *send_rows = route_pack(ids_t, moe_input)
    got_rows = [exchange(half_rows, ALL) for half_rows in send_rows]
    weights = combine_weights(ids_t, route_weights.T)

    queries, _ = lax.optimization_barrier((queries, pick))
    pieces = attention(place, queries, out_grad, keys, values)
    pieces = [p.reshape(N_Z * TOK, 4 * HD) for p in pieces]
    pieces = [pieces[0]] + [ahead_y(pieces[k], k) for k in others]

    w_near, w_far, *pieces = lax.optimization_barrier((w_near, w_far, *pieces))
    swap = [(0, 1), (1, 0)]
    w_mine = [w_own, w_near, w_far]
    w_other = [lax.ppermute(w_near, "section", swap), lax.ppermute(w_far, "section", swap)]

    def head_half(weights):
        parts = project(place, pieces, weights)
        return [parts[0]] + [ahead_z(parts[k], k) for k in others]

    head_mine = head_half(w_mine)
    head_other = head_half(w_other)
    got_grads = exchange(sum_pack(place, head_mine, head_other, resid_grad, pick), ALL)
    w_gu = w_gate_up.reshape(D, 2 * FF)
    factors = gate_factors(got_rows, w_gu)
    back = expert_back(got_grads, factors, w_down.reshape(FF, D), w_gu)
    return combine(exchange(back, ALL), weights)


def solution(mesh):
    return jax.shard_map(
        body,
        mesh=mesh,
        in_specs=(
            P(("section", "col"), "row"),
            P(("section", "col"), None),
            P(("section", "col"), None),
            P(("section", "col"), "row"),
            P("col", "row"),
            P("col", None),
            P("col", None),
            P(ALL, None),
            P(ALL, None),
            P(ALL, None),
            P(ALL, None),
            P(ALL, None, None),
            P(ALL, None, None),
        ),
        out_specs=P(ALL, None),
        check_vma=False,
    )
```

```python
import math

import jax
import jax.numpy as jnp
from jax import lax
from jax.experimental import pallas as pl
from jax.experimental.pallas import tpu as pltpu
from jax.sharding import PartitionSpec as P

HEADS = 32
KV_HEADS = 4
HD = 128
TOPK = 8
DOC = 1024
D = 2048
FF = 768
CAP = 9
TOK = 128
NE = 128
N_Y = 4
N_Z = 4
HALF = 1024
MSG = 72
CHUNK = 32
ROWS = CHUNK * CAP
BF = jnp.bfloat16
F32 = jnp.float32
VMEM_LIMIT = 60 * 1024 * 1024
ALL = ("section", "row", "col")
SCALE = HD ** (-0.5)


def params(steps):
    return pltpu.CompilerParams(
        dimension_semantics=("arbitrary",) * steps, vmem_limit_bytes=VMEM_LIMIT
    )


def cost(us):
    return pl.CostEstimate(flops=int(us * 1.1e9), transcendentals=0, bytes_accessed=int(us * 3e6))


def dot_nn(a, b):
    return lax.dot_general(a, b, (((1,), (0,)), ((), ())), preferred_element_type=F32)


def dot_nt(a, b):
    return lax.dot_general(a, b, (((1,), (1,)), ((), ())), preferred_element_type=F32)


def pack_half(x, pick, out_ref, scr):
    main = pick[: NE * 8]
    last = pick[NE * 8 :]
    for jj in range(0, 8, 2):
        got = dot_nn(main, x[:, jj * 128 : (jj + 2) * 128])
        for q in range(2):
            piece = got[:, q * 128 : (q + 1) * 128].reshape(NE, 8, 128)
            out_ref[:, (jj + q) * 8 : (jj + q + 1) * 8, :] = piece.astype(BF)
    ninth = dot_nn(last, x)
    for jj in range(8):
        scr[pl.ds(jj, NE, stride=8), :] = ninth[:, jj * 128 : (jj + 1) * 128]
    out_ref[:, 64:72, :] = scr[...].reshape(NE, 8, 128).astype(BF)


def slot_tables(ids_ref):
    e_iota = lax.broadcasted_iota(jnp.int32, (NE, TOK), 0)
    named = jnp.zeros((NE, TOK), F32)
    for k in range(TOPK):
        named = named + jnp.where(ids_ref[k : k + 1, :] == e_iota, 1.0, 0.0)
    before = jnp.where(
        lax.broadcasted_iota(jnp.int32, (TOK, TOK), 0)
        < lax.broadcasted_iota(jnp.int32, (TOK, TOK), 1),
        1.0,
        0.0,
    ).astype(BF)
    count = dot_nn(named.astype(BF), before)
    return e_iota, jnp.where(named > 0.5, count, -1.0)


def spread_matrix():
    r = lax.broadcasted_iota(jnp.int32, (NE * 8, NE), 0)
    c = lax.broadcasted_iota(jnp.int32, (NE * 8, NE), 1)
    return jnp.where(lax.shift_right_logical(r, 3) == c, 1.0, 0.0).astype(BF)


def slot_number():
    r = lax.broadcasted_iota(jnp.int32, (NE * 8, TOK), 0)
    return jnp.bitwise_and(r, 7).astype(F32)


def route_pack_kernel(ids_ref, x_ref, pick_ref, out0, out1, scr):
    _, count = slot_tables(ids_ref)
    wide = dot_nn(spread_matrix(), count.astype(BF))
    pick_ref[: NE * 8] = jnp.where(wide == slot_number(), 1.0, 0.0).astype(BF)
    pick_ref[NE * 8 :] = jnp.where(count == 8.0, 1.0, 0.0).astype(BF)
    for n, out in enumerate((out0, out1)):
        pack_half(x_ref[:, n * HALF : (n + 1) * HALF], pick_ref[...], out, scr)


def route_pack(ids_t, x):
    half = jax.ShapeDtypeStruct((NE, MSG, 128), BF)
    return pl.pallas_call(
        route_pack_kernel,
        out_shape=[jax.ShapeDtypeStruct((NE * CAP, TOK), BF), half, half],
        scratch_shapes=[pltpu.VMEM((NE * 8, 128), F32)],
        compiler_params=pltpu.CompilerParams(vmem_limit_bytes=VMEM_LIMIT),
        name="route_pack",
        cost_estimate=cost(5),
    )(ids_t, x)


def weights_kernel(ids_ref, rw_ref, out_ref):
    e_iota, count = slot_tables(ids_ref)
    weight = jnp.zeros((NE, TOK), F32)
    for k in range(TOPK):
        weight = weight + jnp.where(ids_ref[k : k + 1, :] == e_iota, rw_ref[k : k + 1, :], 0.0)
    high = weight.astype(BF)
    low = (weight - high.astype(F32)).astype(BF)
    spread = spread_matrix()
    hit = dot_nn(spread, count.astype(BF)) == slot_number()
    for i, part in enumerate((high, low)):
        wide = jnp.where(hit, dot_nn(spread, part), 0.0)
        out_ref[i * TOK : (i + 1) * TOK, : NE * 8] = wide.T.astype(BF)
        tail = jnp.where(count == 8.0, part.astype(F32), 0.0)
        out_ref[i * TOK : (i + 1) * TOK, NE * 8 :] = tail.T.astype(BF)


def combine_weights(ids_t, rw_t):
    return pl.pallas_call(
        weights_kernel,
        out_shape=jax.ShapeDtypeStruct((2 * TOK, NE * CAP), BF),
        compiler_params=pltpu.CompilerParams(vmem_limit_bytes=VMEM_LIMIT),
        name="combine_weights",
        cost_estimate=cost(2.2),
    )(ids_t, rw_t)


def attention_kernel(
    at_ref, q_ref, g_ref, k_ref, v_ref, out0, out1, out2, out3, dk_acc, dv_acc, out_ref
):
    blk = 256
    factor = SCALE * math.log2(math.e)
    k_all = k_ref[...]
    k_t = k_all.astype(F32).T.astype(BF)
    allowed = lax.broadcasted_iota(jnp.int32, (blk, blk), 0) <= lax.broadcasted_iota(
        jnp.int32, (blk, blk), 1
    )
    first = True
    for h in range(2):
        for qb in reversed(range(DOC // blk)):
            length = (qb + 1) * blk
            q = q_ref[qb * blk : length, h * HD : (h + 1) * HD]
            g = g_ref[qb * blk : length, h * HD : (h + 1) * HD]
            k = k_ref[:length, :]
            v = v_ref[:length, :]
            s = dot_nt(k, q)
            diag = jnp.where(allowed, s[length - blk :], -jnp.inf)
            s = jnp.concatenate([s[: length - blk], diag], axis=0) if qb else diag
            top = jnp.max(s, axis=0, keepdims=True)
            expo = jnp.exp2((s - top) * factor)
            inv = 1.0 / jnp.sum(expo, axis=0, keepdims=True)
            dprob = dot_nt(v, g)
            delta = jnp.sum(expo * dprob, axis=0, keepdims=True) * inv
            probs = expo * inv
            dscore = (probs * (dprob - delta)).astype(BF)
            probs_b = probs.astype(BF)
            dq_t = dot_nn(k_t[:, :length], dscore) * SCALE
            dq = dq_t.T.astype(BF)
            y = (2 * qb) % N_Y
            z = qb // 2
            out_ref[y, z, :, h * HD : (h + 1) * HD] = dq[:128]
            out_ref[y + 1, z, :, h * HD : (h + 1) * HD] = dq[128:]
            dk = dot_nn(dscore, q)
            dv = dot_nn(probs_b, g)
            if first:
                dk_acc[...] = dk
                dv_acc[...] = dv
                first = False
            else:
                dk_acc[:length] += dk
                dv_acc[:length] += dv
    for b in range(DOC // 128):
        out_ref[b % N_Y, b // N_Y, :, 2 * HD : 3 * HD] = (
            dk_acc[b * 128 : (b + 1) * 128, :] * SCALE
        ).astype(BF)
        out_ref[b % N_Y, b // N_Y, :, 3 * HD :] = dv_acc[b * 128 : (b + 1) * 128, :].astype(BF)
    for k, out in enumerate((out0, out1, out2, out3)):
        out[...] = out_ref[jnp.bitwise_and(at_ref[1] + k, N_Y - 1)]


def attention(place, queries, out_grad, keys, values):
    docs = queries.shape[0] // DOC
    wide = pl.BlockSpec((DOC, 2 * HD), lambda d, at: (d, 0))
    thin = pl.BlockSpec((DOC, HD), lambda d, at: (d, at[0]))
    piece = pl.BlockSpec((N_Z // docs, TOK, 4 * HD), lambda d, at: (d, 0, 0))
    return pl.pallas_call(
        attention_kernel,
        grid_spec=pltpu.PrefetchScalarGridSpec(
            num_scalar_prefetch=1,
            grid=(docs,),
            in_specs=[wide, wide, thin, thin],
            out_specs=[piece] * N_Y,
            scratch_shapes=[
                pltpu.VMEM((DOC, HD), F32),
                pltpu.VMEM((DOC, HD), F32),
                pltpu.VMEM((N_Y, N_Z // docs, TOK, 4 * HD), BF),
            ],
        ),
        out_shape=[jax.ShapeDtypeStruct((N_Z, TOK, 4 * HD), BF)] * N_Y,
        compiler_params=params(1),
        name="attention",
        cost_estimate=cost(16),
    )(place, queries, out_grad, keys, values)


def project_kernel(at_ref, x0, x1, x2, x3, *refs):
    *weights, out0, out1, out2, out3, scr = refs
    pieces = (x0, x1, x2, x3)
    total = x0[:, 2 * HD :].astype(F32)
    for x in pieces[1:]:
        total = total + x[:, 2 * HD :].astype(F32)
    total = total.astype(BF)
    width = scr.shape[3]
    unit = 0
    for w_ref in weights:
        for h in range(w_ref.shape[0]):
            acc = dot_nt(total, w_ref[h, N_Y * width :])
            for y, x in enumerate(pieces):
                acc = acc + dot_nt(x[:, : 2 * HD], w_ref[h, y * width : (y + 1) * width])
            for z in range(N_Z):
                scr[z, unit] = acc[z * TOK : (z + 1) * TOK].astype(BF)
            unit += 1
    for k, out in enumerate((out0, out1, out2, out3)):
        out[...] = scr[jnp.bitwise_and(at_ref[0] + k, N_Z - 1)]


def project(place, pieces, weights):
    width = weights[0].shape[1] // (N_Y + 1)
    units = sum(w.shape[0] for w in weights)
    whole = pl.BlockSpec(memory_space=pltpu.VMEM)
    return pl.pallas_call(
        project_kernel,
        in_specs=[pl.BlockSpec(memory_space=pltpu.SMEM)] + [whole] * (N_Y + len(weights)),
        out_specs=[whole] * N_Z,
        out_shape=[jax.ShapeDtypeStruct((units, TOK, width), BF)] * N_Z,
        scratch_shapes=[pltpu.VMEM((N_Z, units, TOK, width), BF)],
        compiler_params=pltpu.CompilerParams(vmem_limit_bytes=VMEM_LIMIT),
        name="project",
        cost_estimate=cost(0.6 * units),
    )(place, *pieces, *weights)


def sum_pack_kernel(at_ref, m0, m1, m2, m3, o0, o1, o2, o3, resid_ref, pick_ref, out_ref, sums, scr):
    @pl.when(pl.program_id(0) == 0)
    def _():
        mine = m0.shape[0]
        for u in range(mine):
            sums[u] = sum((x[u].astype(F32) for x in (m1, m2, m3)), m0[u].astype(F32))
        for u in range(o0.shape[0]):
            sums[mine + u] = sum((x[u].astype(F32) for x in (o1, o2, o3)), o0[u].astype(F32))

    section, col = at_ref[2], at_ref[3]
    blocks = []
    for c in range(2):
        behind = jnp.bitwise_and(2 * pl.program_id(0) + c - col, 3)
        for h in range(2):
            far = jnp.where(section == h, 4, 7)
            near = jnp.where(behind == jnp.where(section == 0, 3, 1), 2 + h, 5 + h)
            unit = jnp.where(behind == 0, h, jnp.where(behind == 2, far, near))
            blocks.append(sums[unit])
    total = resid_ref[...].astype(F32) + jnp.concatenate(blocks, axis=1)
    pack_half(total.astype(BF), pick_ref[...], out_ref, scr)


def sum_pack(place, mine, other, resid, pick):
    def whole(x):
        return pl.BlockSpec(x.shape, lambda n, at: (0, 0, 0))

    units = mine[0].shape[0] + other[0].shape[0]
    return pl.pallas_call(
        sum_pack_kernel,
        grid_spec=pltpu.PrefetchScalarGridSpec(
            num_scalar_prefetch=1,
            grid=(2,),
            in_specs=[whole(x) for x in (*mine, *other)]
            + [
                pl.BlockSpec((TOK, HALF), lambda n, at: (0, n)),
                pl.BlockSpec((NE * CAP, TOK), lambda n, at: (0, 0)),
            ],
            out_specs=pl.BlockSpec((NE, MSG, 128), lambda n, at: (0, n, 0)),
            scratch_shapes=[
                pltpu.VMEM((units, TOK, 256), F32),
                pltpu.VMEM((NE * 8, 128), F32),
            ],
        ),
        out_shape=jax.ShapeDtypeStruct((NE, 2 * MSG, 128), BF),
        compiler_params=params(1),
        name="sum_pack",
        cost_estimate=cost(4),
    )(place, *mine, *other, resid, pick)


def unpack_rows(halves, rows, scr):
    main = CHUNK * 8
    for n, msg_ref in enumerate(halves):
        scr[...] = msg_ref[:, 64:, :].astype(F32).reshape(main, 128)
        for jj in range(8):
            at = (n * 8 + jj) * 128
            piece = msg_ref[:, jj * 8 : (jj + 1) * 8, :]
            rows[:main, at : at + 128] = piece.reshape(main, 128)
            rows[main:, at : at + 128] = scr[pl.ds(jj, CHUNK, stride=8), :].astype(BF)


def gate_up_kernel(msg0, msg1, w_ref, out_ref, rows, scr):
    unpack_rows((msg0, msg1), rows, scr)
    gate_up = dot_nn(rows[...], w_ref[...])
    gate = gate_up[:, :FF]
    up = gate_up[:, FF:]
    sigm = 1.0 / (1.0 + jnp.exp(-gate))
    out_ref[:, :FF] = (up * sigm * (1.0 + gate * (1.0 - sigm))).astype(BF)
    out_ref[:, FF:] = (gate * sigm).astype(BF)


def gate_factors(halves, w_gu):
    steps = NE // CHUNK
    return pl.pallas_call(
        gate_up_kernel,
        grid=(steps,),
        in_specs=[
            pl.BlockSpec((CHUNK, MSG, 128), lambda i: (i, 0, 0)),
            pl.BlockSpec((CHUNK, MSG, 128), lambda i: (i, 0, 0)),
            pl.BlockSpec((D, 2 * FF), lambda i: (0, 0)),
        ],
        out_specs=pl.BlockSpec((ROWS, 2 * FF), lambda i: (i, 0)),
        out_shape=jax.ShapeDtypeStruct((NE * CAP, 2 * FF), BF),
        scratch_shapes=[pltpu.VMEM((ROWS, D), BF), pltpu.VMEM((CHUNK * 8, 128), F32)],
        compiler_params=params(1),
        name="gate_factors",
        cost_estimate=cost(12.5),
    )(*halves, w_gu)


def expert_kernel(msg0, msg1, fac_ref, wd_ref, w_ref, out_ref, rows, scr):
    main = CHUNK * 8
    unpack_rows((msg0, msg1), rows, scr)
    dhidden = dot_nt(rows[...], wd_ref[...])
    d_gate = (dhidden * fac_ref[:, :FF].astype(F32)).astype(BF)
    d_up = (dhidden * fac_ref[:, FF:].astype(F32)).astype(BF)
    both = jnp.concatenate([d_gate, d_up], axis=1)
    for n in range(2):
        back = dot_nt(both, w_ref[n * HALF : (n + 1) * HALF, :])
        for jj in range(8):
            piece = back[:main, jj * 128 : (jj + 1) * 128].reshape(CHUNK, 8, 128)
            out_ref[:, n * MSG + jj * 8 : n * MSG + (jj + 1) * 8, :] = piece.astype(BF)
            scr[pl.ds(jj, CHUNK, stride=8), :] = back[main:, jj * 128 : (jj + 1) * 128]
        out_ref[:, n * MSG + 64 : (n + 1) * MSG, :] = scr[...].reshape(CHUNK, 8, 128).astype(BF)


def expert_back(msg, factors, w_dn, w_gu):
    steps = NE // CHUNK
    return pl.pallas_call(
        expert_kernel,
        grid=(steps,),
        in_specs=[
            pl.BlockSpec((CHUNK, MSG, 128), lambda i: (i, 0, 0)),
            pl.BlockSpec((CHUNK, MSG, 128), lambda i: (i, 1, 0)),
            pl.BlockSpec((ROWS, 2 * FF), lambda i: (i, 0)),
            pl.BlockSpec((FF, D), lambda i: (0, 0)),
            pl.BlockSpec((D, 2 * FF), lambda i: (0, 0)),
        ],
        out_specs=pl.BlockSpec((CHUNK, 2 * MSG, 128), lambda i: (i, 0, 0)),
        out_shape=jax.ShapeDtypeStruct((NE, 2 * MSG, 128), BF),
        scratch_shapes=[pltpu.VMEM((ROWS, D), BF), pltpu.VMEM((CHUNK * 8, 128), F32)],
        compiler_params=params(1),
        name="expert_back",
        cost_estimate=cost(20),
    )(msg, msg, factors, w_dn, w_gu)


def combine_kernel(msg_ref, w_ref, out_ref, scr):
    scr[...] = msg_ref[:, 64:72, :].astype(F32).reshape(NE * 8, 128)
    w_main = w_ref[:, : NE * 8]
    w_last = w_ref[:, NE * 8 :]
    for jj in range(0, 8, 2):
        pair = range(jj, jj + 2)
        piece = jnp.concatenate(
            [msg_ref[:, q * 8 : (q + 1) * 8, :].reshape(NE * 8, 128) for q in pair], axis=1
        )
        ninth = jnp.concatenate([scr[pl.ds(q, NE, stride=8), :].astype(BF) for q in pair], axis=1)
        both = dot_nn(w_main, piece) + dot_nn(w_last, ninth)
        out_ref[:, jj * 128 : (jj + 2) * 128] = (both[:TOK] + both[TOK:]).astype(BF)


def combine(msg, weights):
    return pl.pallas_call(
        combine_kernel,
        grid=(2,),
        in_specs=[
            pl.BlockSpec((NE, MSG, 128), lambda n: (0, n, 0)),
            pl.BlockSpec((2 * TOK, NE * CAP), lambda n: (0, 0)),
        ],
        out_specs=pl.BlockSpec((TOK, HALF), lambda n: (0, n)),
        out_shape=jax.ShapeDtypeStruct((TOK, D), BF),
        scratch_shapes=[pltpu.VMEM((NE * 8, 128), F32)],
        compiler_params=params(1),
        name="combine",
        cost_estimate=cost(5.3),
    )(msg, weights)


def exchange(x, axis, groups=None):
    return lax.all_to_all(
        x, axis, split_axis=0, concat_axis=0, tiled=True, axis_index_groups=groups
    )


def body(
    queries,
    keys,
    values,
    out_grad,
    q_weight,
    k_weight,
    v_weight,
    resid_grad,
    moe_input,
    expert_ids,
    route_weights,
    w_gate_up,
    w_down,
):
    n_col = lax.axis_size("col")
    row = lax.axis_index("row")
    kv_index = row // N_Y
    section = lax.axis_index("section")
    place = jnp.stack([kv_index, row % N_Y, section, lax.axis_index("col")]).astype(jnp.int32)
    others = range(1, N_Y)

    def ahead_y(x, k):
        hops = [(N_Y * z + y, N_Y * z + (y + k) % N_Y) for z in range(N_Z) for y in range(N_Y)]
        return lax.ppermute(x, "row", hops)

    def ahead_z(x, k):
        hops = [(N_Y * z + y, N_Y * ((z + k) % N_Z) + y) for z in range(N_Z) for y in range(N_Y)]
        return lax.ppermute(x, "row", hops)

    half = D // n_col // 2
    wk = lax.dynamic_slice_in_dim(k_weight, kv_index * HD, HD, 1)
    wv = lax.dynamic_slice_in_dim(v_weight, kv_index * HD, HD, 1)
    w_own = jnp.concatenate(
        [
            w.reshape(2, half, 2 * HD)
            for w in (
                q_weight,
                *(ahead_y(q_weight, k) for k in others),
                jnp.concatenate([wk, wv], axis=1),
            )
        ],
        axis=1,
    )
    near_hops = [(c, (c + 1) % n_col) for c in range(n_col)]
    near_hops += [(n_col + c, n_col + (c - 1) % n_col) for c in range(n_col)]
    w_near = lax.ppermute(w_own, ("section", "col"), near_hops)
    w_far = lax.ppermute(
        lax.dynamic_slice_in_dim(w_own, section, 1, 0),
        "col",
        [(c, (c + 2) % n_col) for c in range(n_col)],
    )

    ids_t = expert_ids.T
    pick, *send_rows = route_pack(ids_t, moe_input)
    got_rows = [exchange(half_rows, ALL) for half_rows in send_rows]
    weights = combine_weights(ids_t, route_weights.T)

    queries, _ = lax.optimization_barrier((queries, pick))
    pieces = attention(place, queries, out_grad, keys, values)
    pieces = [p.reshape(N_Z * TOK, 4 * HD) for p in pieces]
    pieces = [pieces[0]] + [ahead_y(pieces[k], k) for k in others]

    w_near, w_far, *pieces = lax.optimization_barrier((w_near, w_far, *pieces))
    swap = [(0, 1), (1, 0)]
    w_mine = [w_own, w_near, w_far]
    w_other = [lax.ppermute(w_near, "section", swap), lax.ppermute(w_far, "section", swap)]

    def head_half(weights):
        parts = project(place, pieces, weights)
        return [parts[0]] + [ahead_z(parts[k], k) for k in others]

    head_mine = head_half(w_mine)
    head_other = head_half(w_other)
    got_grads = exchange(sum_pack(place, head_mine, head_other, resid_grad, pick), ALL)
    w_gu = w_gate_up.reshape(D, 2 * FF)
    factors = gate_factors(got_rows, w_gu)
    back = expert_back(got_grads, factors, w_down.reshape(FF, D), w_gu)
    return combine(exchange(back, ALL), weights)


def solution(mesh):
    return jax.shard_map(
        body,
        mesh=mesh,
        in_specs=(
            P(("section", "col"), "row"),
            P(("section", "col"), None),
            P(("section", "col"), None),
            P(("section", "col"), "row"),
            P("col", "row"),
            P("col", None),
            P("col", None),
            P(ALL, None),
            P(ALL, None),
            P(ALL, None),
            P(ALL, None),
            P(ALL, None, None),
            P(ALL, None, None),
        ),
        out_specs=P(ALL, None),
        check_vma=False,
    )
```
